32 devices in a mesh: ctx: 8 (over z, y), dp: 4 (over x, core).
Axes of the slice: x: 2, y: 2, z: 4, core: 2. Of those that a mesh axis runs over, the one named last changes fastest.
Arguments:
- tokens: bfloat16 [8, 1024, 1536], P('dp', 'ctx'), may hold values from -6 to 6
- block_pair: int32 [8], replicated, may hold values from 0 to 7, each once
- gain_attn: bfloat16 [1536], P('dp'), may hold values from 0.099609375 to 1.8984375
- w_query: bfloat16 [1536, 1536], P('dp'), may hold values from -0.15625 to 0.15625
- b_query: bfloat16 [1536], P('dp'), may hold values from -2.5 to 2.5
- w_key: bfloat16 [1536, 256], P('dp'), may hold values from -0.15625 to 0.15625
- b_key: bfloat16 [256], P('dp'), may hold values from -2.5 to 2.5
- w_value: bfloat16 [1536, 256], P('dp'), may hold values from -0.15625 to 0.15625
- b_value: bfloat16 [256], P('dp'), may hold values from -0.59765625 to 0.59765625
- w_out: bfloat16 [1536, 1536], P('dp'), may hold values from -0.875 to 0.875
- gain_mlp: bfloat16 [1536], P('dp'), may hold values from 0.099609375 to 1.8984375
- w_gate: bfloat16 [1536, 8960], P(None, 'dp'), may hold values from -0.15625 to 0.15625
- w_up: bfloat16 [1536, 8960], P(None, 'dp'), may hold values from -0.15625 to 0.15625
- w_down: bfloat16 [8960, 1536], P('dp'), may hold values from -0.0625 to 0.0625
- cotangent: bfloat16 [8, 1024, 1536], P('dp', 'ctx'), may hold values from -6 to 6
Outputs:
- layer_out: bfloat16 [8, 1024, 1536], P('dp', 'ctx')
- grad_input: float32 [8, 1024, 1536], P('dp', 'ctx')
- grad_gain_attn: float32 [1536], P('dp')
- grad_w_query: float32 [1536, 1536], P('dp')
- grad_b_query: float32 [1536], P('dp')
- grad_w_key: float32 [1536, 256], P('dp')
- grad_b_key: float32 [256], P('dp')
- grad_w_value: float32 [1536, 256], P('dp')
- grad_b_value: float32 [256], P('dp')
- grad_w_out: float32 [1536, 1536], P('dp')
- grad_gain_mlp: float32 [1536], P('dp')
- grad_w_gate: float32 [1536, 8960], P(None, 'dp')
- grad_w_up: float32 [1536, 8960], P(None, 'dp')
- grad_w_down: float32 [8960, 1536], P('dp')
The draws below stay inside these ranges and needn't reach their ends.
Inputs may be any that keep to these rules, and one draw needn't show every extreme that they name: A permutation; index c of ctx holds blocks block_pair[c] and 15 - block_pair[c] of every sequence.
All inputs are finite; a program needn't handle non-finite values.
Results may differ from the reference program's by a relative error of at most 0.02.
Values may be sent and summed in bfloat16 or wider, within the bound.
No kernel may reach another device: no remote copies, remote signals or barrier semaphores. Data moves between devices by JAX's collectives and lax.ppermute only.
A program may use at most 512 MiB of HBM per device.

```python
import math
import jax
import jax.numpy as jnp
from jax import lax

D = 1536
FF = 8960
HEADS = 12
KV_HEADS = 2
HEAD = 128
SEQ_TOK = 128
KVD = 256
GROUP = 6
BLK = 64
SEQ_LEN = 1024
SEQS = 8
N_CTX = 8


def level_of(rng, extent, pieces, least, high):
    loudness, own = 1.0, jax.random.fold_in(rng, 6)
    for position, shards_of in pieces:
        draws = jnp.exp(jax.random.uniform(jax.random.fold_in(own, position), (shards_of,), jnp.float32, least / len(pieces), high / len(pieces)))
        loudness = loudness * jnp.repeat(draws, extent[position] // shards_of).reshape([-1 if axis == position else 1 for axis in range(len(extent))])
    return loudness


def scatter_about(own_key, dims, deviation, limit, split=(), held_as=jnp.bfloat16):
    array = jax.random.normal(own_key, dims, jnp.float32) * deviation
    if len(split) > 0:
        array = level_of(own_key, dims, split, -0.22, 0.18) * array
    return jnp.clip(array, min=-limit, max=limit).astype(held_as)


def setup_inputs(seed: int = 0) -> dict:
    keys = jax.random.split(jax.random.key(seed), 16)
    return {
        "tokens": scatter_about(keys[0], (SEQS, SEQ_LEN, D), 1.0, 6.0, ((0, 4), (1, 8))),
        "block_pair": jax.random.permutation(keys[1], N_CTX).astype(jnp.int32),
        "gain_attn": jnp.clip(1.0 + 0.18 * jax.random.normal(keys[2], (D,), jnp.float32), 0.099609375, 1.8984375).astype(jnp.bfloat16),
        "w_query": scatter_about(keys[3], (D, D), D ** -0.5, 0.15625, ((0, 4),)),
        "b_query": scatter_about(keys[4], (D,), 0.5, 2.5, ((0, 4),)),
        "w_key": scatter_about(keys[5], (D, KVD), D ** -0.5, 0.15625, ((0, 4),)),
        "b_key": scatter_about(keys[6], (KVD,), 0.5, 2.5, ((0, 4),)),
        "w_value": scatter_about(keys[7], (D, KVD), D ** -0.5, 0.15625, ((0, 4),)),
        "b_value": scatter_about(keys[8], (KVD,), 0.1, 0.59765625, ((0, 4),)),
        "w_out": scatter_about(keys[9], (D, D), (D // 32) ** -0.5, 0.875, ((0, 4),)),
        "gain_mlp": jnp.clip(1.0 + 0.18 * jax.random.normal(keys[10], (D,), jnp.float32), 0.099609375, 1.8984375).astype(jnp.bfloat16),
        "w_gate": scatter_about(keys[11], (D, FF), D ** -0.5, 0.15625, ((1, 4),)),
        "w_up": scatter_about(keys[12], (D, FF), D ** -0.5, 0.15625, ((1, 4),)),
        "w_down": scatter_about(keys[13], (FF, D), FF ** -0.5, 0.0625, ((0, 4),)),
        "cotangent": scatter_about(keys[14], (SEQS, SEQ_LEN, D), 1.0, 6.0, ((0, 4), (1, 8))),
    }


EPSILON = 1e-06
THETA = 1000000.0
HIGHEST = lax.Precision.HIGHEST

@jax.custom_vjp
def low(v):
    return lax.optimization_barrier(v.astype(jnp.bfloat16)).astype(jnp.float32)

@jax.custom_vjp
def low_back(v):
    return v

def low_keep(v):
    return (low(v), None)

def low_pass(kept, grad):
    return (grad,)

def back_keep(v):
    return (v, None)

def back_low(kept, grad):
    return (low(grad),)
low.defvjp(low_keep, low_pass)
low_back.defvjp(back_keep, back_low)

def block_positions(block_pair):
    row_ids = jnp.arange(SEQ_LEN, dtype=jnp.int32)
    owner = row_ids // SEQ_TOK
    within = row_ids % SEQ_TOK
    first = block_pair[owner]
    chosen = jnp.where(within < BLK, first, 2 * N_CTX - 1 - first)
    return (chosen * BLK + within % BLK).astype(jnp.int32)

def angles_for(positions):
    half_size = HEAD // 2
    freqs = jnp.exp(jnp.arange(half_size, dtype=jnp.float32) * (-math.log(THETA) / half_size))
    angle = positions.astype(jnp.float32)[:, None] * freqs[None, :]
    return (jnp.cos(angle), jnp.sin(angle))

def rotate(vectors, cosine, sine):
    half_size = vectors.shape[-1] // 2
    front = vectors[..., :half_size]
    behind = vectors[..., half_size:]
    return jnp.concatenate([front * cosine - behind * sine, behind * cosine + front * sine], -1)

def rms_norm(vectors, gain):
    return vectors * lax.rsqrt(lax.optimization_barrier(jnp.mean(vectors * vectors, -1, keepdims=True)) + EPSILON) * gain

def product(left, right):
    return jnp.dot(left, right, precision=HIGHEST, preferred_element_type=jnp.float32)

def attention(queries, key_rows, value_rows, positions):
    block_rows = min(512, SEQ_LEN)
    block_count = SEQ_LEN // block_rows
    grouped = queries.reshape(block_count, block_rows, KV_HEADS, GROUP, HEAD)
    query_pos = positions.reshape(block_count, block_rows)

    def one_block(items):
        block, block_pos = items
        scores = low_back(jnp.einsum('qkgd,nkd->kgqn', block, key_rows, precision=HIGHEST) * HEAD ** (-0.5))
        allowed = positions[None, :] <= block_pos[:, None]
        scores = jnp.where(allowed[None, None], scores, -jnp.inf)
        probs = low(jax.nn.softmax(scores, -1))
        mixed = jnp.einsum('kgqn,nkd->qkgd', probs, value_rows, precision=HIGHEST)
        return mixed.reshape(block_rows, D)
    return lax.map(jax.checkpoint(one_block), (grouped, query_pos)).reshape(SEQ_LEN, D)

def layer(inputs, positions, gain_attn, w_query, b_query, w_key, b_key, w_value, b_value, w_out, gain_mlp, w_gate, w_up, w_down):
    cosine, sine = angles_for(positions)
    cosine = cosine[:, None, :]
    sine = sine[:, None, :]
    normed_one = low(rms_norm(inputs, gain_attn))
    query_pre = low_back(product(normed_one, w_query) + b_query)
    key_pre = low_back(product(normed_one, w_key) + b_key)
    value_pre = low_back(product(normed_one, w_value) + b_value)
    queries = low(rotate(query_pre.reshape(SEQ_LEN, HEADS, HEAD), cosine, sine))
    key_rows = low(rotate(key_pre.reshape(SEQ_LEN, KV_HEADS, HEAD), cosine, sine))
    value_rows = low(value_pre.reshape(SEQ_LEN, KV_HEADS, HEAD))
    mixed = attention(queries, key_rows, value_rows, positions)
    attn_vec = low(low_back(mixed))
    middle = inputs + low_back(product(attn_vec, w_out))
    normed_two = low(rms_norm(middle, gain_mlp))
    gate = low_back(product(normed_two, w_gate))
    up_proj = low_back(product(normed_two, w_up))
    hidden = low(jax.nn.silu(gate) * up_proj)
    return middle + product(hidden, w_down)

def reference(tokens, block_pair, gain_attn, w_query, b_query, w_key, b_key, w_value, b_value, w_out, gain_mlp, w_gate, w_up, w_down, cotangent):
    positions = block_positions(block_pair)
    weights = tuple((item.astype(jnp.float32) for item in (gain_attn, w_query, b_query, w_key, b_key, w_value, b_value, w_out, gain_mlp, w_gate, w_up, w_down)))

    def apply(values, *params):
        return layer(values, positions, *params)

    def one_sequence(totals, item):
        seq_in, seq_cot = item
        result, pull = jax.vjp(apply, seq_in.astype(jnp.float32), *weights)
        grads = pull(seq_cot.astype(jnp.float32))
        summed = tuple((left + right for left, right in zip(totals, grads[1:])))
        return (summed, (result.astype(jnp.bfloat16), grads[0]))
    zeros = tuple((jnp.zeros(item.shape, jnp.float32) for item in weights))
    totals, outputs = lax.scan(one_sequence, zeros, (tokens, cotangent))
    layer_out, grad_input = outputs
    return (layer_out, grad_input, totals[0], totals[1], totals[2], totals[3], totals[4], totals[5], totals[6], totals[7], totals[8], totals[9], totals[10], totals[11])
```

```python
import functools
import math

import jax
import jax.numpy as jnp
from jax import lax
from jax.experimental import pallas as pl
from jax.experimental.pallas import tpu as pltpu
from jax.sharding import PartitionSpec as P

HEADS = 12
KV_HEADS = 2
HEAD = 128
GROUP = HEADS // KV_HEADS

EPSILON = 1e-06
THETA = 1000000.0
BF = jnp.bfloat16
F32 = jnp.float32


def matmul(left, right, left_dim, right_dim):
    return lax.dot_general(
        left, right, (((left_dim,), (right_dim,)), ((), ())), preferred_element_type=F32
    )


def dot_nt(left, right):
    return matmul(left, right, 1, 1)


def dot_tn(left, right):
    return matmul(left, right, 0, 0)


def dot_nn(left, right):
    return matmul(left, right, 1, 0)


def block_positions(block_pair, n_ctx, seq_tok):
    half_blk = seq_tok // 2
    row_ids = jnp.arange(n_ctx * seq_tok, dtype=jnp.int32)
    owner = row_ids // seq_tok
    within = row_ids % seq_tok
    matches = owner[:, None] == jnp.arange(n_ctx, dtype=jnp.int32)[None, :]
    first = jnp.sum(jnp.where(matches, block_pair[None, :], 0), 1)
    chosen = jnp.where(within < half_blk, first, 2 * n_ctx - 1 - first)
    return chosen * half_blk + within % half_blk


def rope_tables(positions):
    half_size = HEAD // 2
    freqs = jnp.exp(jnp.arange(half_size, dtype=F32) * (-math.log(THETA) / half_size))
    angle = positions.astype(F32)[:, None] * freqs[None, :]
    cosine, sine = jnp.cos(angle), jnp.sin(angle)
    return jnp.concatenate([cosine, cosine, -sine, sine], 1)


def call(kernel, name, args, specs, outs, out_specs=None, grid=(), flops=0, exps=0, scratch=()):
    size = sum(math.prod(a.shape) * a.dtype.itemsize for a in list(args) + list(outs))
    if out_specs is None:
        out_specs = [whole(o) for o in outs]
    return pl.pallas_call(
        kernel,
        grid=grid,
        in_specs=specs,
        out_specs=out_specs,
        out_shape=outs,
        scratch_shapes=scratch,
        cost_estimate=pl.CostEstimate(flops=flops, transcendentals=exps, bytes_accessed=size),
        name=name,
    )(*args)


SCALARS = pl.BlockSpec(memory_space=pltpu.SMEM)


def whole(array):
    zeros = (0,) * len(array.shape)
    return pl.BlockSpec(array.shape, lambda *_: zeros)


def fixed(array):
    zeros = (0,) * len(array.shape)
    return pl.BlockSpec(array.shape, lambda *_: zeros, pipeline_mode=pl.Buffered(1))


def shape(dims, dtype):
    return jax.ShapeDtypeStruct(tuple(dims), dtype)


def lanes(ref, start, size):
    return ref.at[:, pl.ds(pl.multiple_of(start * size, 128), size)]


def scale_of(x):
    return lax.rsqrt(jnp.mean(x * x, -1, keepdims=True) + EPSILON)


def turn(x, table, sign):
    tables = jnp.concatenate([table] * (x.shape[0] // table.shape[0]), 0)
    return x * tables[:, :HEAD] + sign * (pltpu.roll(x, HEAD // 2, 1) * tables[:, HEAD:])


def norm_kv_kernel(n, seq, at, tok, gain, bias, table, *refs):
    weights, (normed, kv) = refs[:n], refs[n:]
    x = tok[...].astype(F32)
    normed[...] = (x * scale_of(x) * gain[...]).astype(BF)
    part = weights[0].shape[0]
    acc = bias[...]
    for p in range(n):
        acc = acc + dot_nn(lanes(normed, at[2 + p], part)[...], weights[p][...])
    toks = x.shape[0] // seq
    for k in range(KV_HEADS):
        key = turn(acc[:, k * HEAD : (k + 1) * HEAD], table[...], 1.0).astype(BF)
        value = acc[:, (KV_HEADS + k) * HEAD : (KV_HEADS + k + 1) * HEAD].astype(BF)
        for s in range(seq):
            kv[s, k, :, :HEAD] = key[s * toks : (s + 1) * toks]
            kv[s, k, :, HEAD:] = value[s * toks : (s + 1) * toks]


def query_kernel(n, at, normed, bias, table, *refs):
    weights, (out,) = refs[:n], refs[n:]
    part = weights[0].shape[0]
    acc = bias[...]
    for p in range(n):
        acc = acc + dot_nn(lanes(normed, at[2 + p], part)[...], weights[p][...])
    for h in range(HEADS):
        cols = slice(h * HEAD, (h + 1) * HEAD)
        out[:, cols] = turn(acc[:, cols], table[...], 1.0).astype(BF)


def stack_heads(ref):
    return jnp.concatenate([ref[:, g * HEAD : (g + 1) * HEAD] for g in range(GROUP)], 0)


def softmax_of(q, k, qpos, kpos):
    scores = dot_nt(q, k) * (HEAD**-0.5)
    allowed = kpos <= jnp.concatenate([qpos] * GROUP, 0)
    scores = jnp.where(allowed, scores, -jnp.inf)
    expon = jnp.exp(scores - jnp.max(scores, -1, keepdims=True))
    return expon / jnp.sum(expon, -1, keepdims=True)


def attend_forward_kernel(q_ref, kv_ref, qpos, kpos, out_ref):
    rows = q_ref.shape[0]
    keys = kv_ref.shape[0] * kv_ref.shape[1]
    k = kv_ref[:, :, :HEAD].reshape(keys, HEAD)
    v = kv_ref[:, :, HEAD:].reshape(keys, HEAD)
    probs = softmax_of(stack_heads(q_ref), k, qpos[...], kpos[...]).astype(BF)
    mixed = dot_nn(probs, v).astype(BF)
    for g in range(GROUP):
        out_ref[:, g * HEAD : (g + 1) * HEAD] = mixed[g * rows : (g + 1) * rows]


def attention_specs(kv_all):
    n_ctx, _, _, seq_tok, _ = kv_all.shape
    rows = pl.BlockSpec((seq_tok, GROUP * HEAD), lambda s, k: (s, k))
    kv = pl.BlockSpec((n_ctx, None, None, seq_tok, 2 * HEAD), lambda s, k: (0, s, k, 0, 0))
    return rows, kv


def attend_forward(queries, kv_all, qpos, kpos):
    rows, kv = attention_specs(kv_all)
    keys = kv_all.shape[0] * kv_all.shape[3]
    return call(
        attend_forward_kernel,
        "attend_forward",
        (queries, kv_all, qpos, kpos),
        [rows, kv, whole(qpos), whole(kpos)],
        [shape(queries.shape, BF)],
        [rows],
        (kv_all.shape[1], KV_HEADS),
        4 * queries.size * keys,
        queries.shape[0] * HEADS * keys,
    )[0]


def attend_backward_kernel(q_ref, kv_ref, go_ref, qpos, kpos, table, gq_ref, gkv_ref):
    rows = q_ref.shape[0]
    n_ctx, seq_tok, _ = kv_ref.shape
    keys = n_ctx * seq_tok
    scale = HEAD**-0.5
    k = kv_ref[:, :, :HEAD].reshape(keys, HEAD)
    v = kv_ref[:, :, HEAD:].reshape(keys, HEAD)
    q = stack_heads(q_ref)
    go = stack_heads(go_ref)
    probs = softmax_of(q, k, qpos[...], kpos[...])
    gkv_ref[:, :, HEAD:] = dot_tn(probs.astype(BF), go).astype(BF).reshape(n_ctx, seq_tok, HEAD)
    grad_probs = dot_nt(go, v)
    centre = jnp.sum(probs * grad_probs, -1, keepdims=True)
    grad_scores = (probs * (grad_probs - centre)).astype(BF)
    gq = turn(dot_nn(grad_scores, k) * scale, table[...], -1.0).astype(BF)
    for g in range(GROUP):
        gq_ref[:, g * HEAD : (g + 1) * HEAD] = gq[g * rows : (g + 1) * rows]
    gk = dot_tn(grad_scores, q) * scale
    gkv_ref[:, :, :HEAD] = gk.astype(BF).reshape(n_ctx, seq_tok, HEAD)


def attend_backward(queries, kv_all, grad_mixed, qpos, kpos, table):
    rows, kv = attention_specs(kv_all)
    keys = kv_all.shape[0] * kv_all.shape[3]
    return call(
        attend_backward_kernel,
        "attend_backward",
        (queries, kv_all, grad_mixed, qpos, kpos, table),
        [rows, kv, rows, whole(qpos), whole(kpos), whole(table)],
        [shape(queries.shape, BF), shape(kv_all.shape, BF)],
        [rows, kv],
        (kv_all.shape[1], KV_HEADS),
        10 * queries.size * keys,
        queries.shape[0] * HEADS * keys,
    )


def out_norm_kernel(n, at, tok, attn, gain, *refs):
    weights, (middle, normed) = refs[:n], refs[n:]
    part = weights[0].shape[0]
    acc = tok[...].astype(F32)
    for p in range(n):
        acc = acc + dot_nn(lanes(attn, at[2 + p], part)[...], weights[p][...])
    middle[...] = acc
    normed[...] = (acc * scale_of(acc) * gain[...]).astype(BF)


def hidden_back_kernel(n, wd, *refs):
    rows, out = refs[:n], refs[n]
    step = rows[0].shape[0]
    for p in range(n):
        out[:, p * step : (p + 1) * step] = dot_nt(wd[...], rows[p][...]).astype(BF)


def unit_tile(total):
    return max(t for t in range(16, 513, 16) if total % t == 0)


def hidden_back(w_down, blocks):
    n = len(blocks)
    rows, width = blocks[0].shape
    wide = w_down.shape[0]
    tile = unit_tile(wide)
    return call(
        functools.partial(hidden_back_kernel, n),
        "hidden_back",
        (w_down, *blocks),
        [pl.BlockSpec((tile, width), lambda i: (i, 0))] + [fixed(b) for b in blocks],
        [shape((wide, n * rows), BF)],
        [pl.BlockSpec((tile, n * rows), lambda i: (i, 0))],
        (wide // tile,),
        2 * n * rows * width * wide,
    )[0]


def units_kernel(n, gh, wg, wu, *refs):
    rows, (hidden, gg, gu) = refs[:n], refs[n:]
    step = rows[0].shape[0]
    for p in range(n):
        cols = slice(p * step, (p + 1) * step)
        gate = dot_nt(wg[...], rows[p][...])
        up = dot_nt(wu[...], rows[p][...])
        grad = gh[:, cols].astype(F32)
        sigma = 1.0 / (1.0 + jnp.exp(-gate))
        act = gate * sigma
        hidden[:, cols] = (act * up).astype(BF)
        gu[:, cols] = (grad * act).astype(BF)
        gg[:, cols] = (grad * up * sigma * (1.0 + gate - act)).astype(BF)


def units(grad_hidden, first, w_gate, w_up, blocks):
    n = len(blocks)
    rows, width = blocks[0].shape
    wide = w_gate.shape[0]
    tile = unit_tile(wide)
    weight = pl.BlockSpec((tile, width), lambda i: (i, 0))
    out = pl.BlockSpec((tile, n * rows), lambda i: (i, 0))
    return call(
        functools.partial(units_kernel, n),
        "units",
        (grad_hidden, w_gate, w_up, *blocks),
        [pl.BlockSpec((tile, n * rows), lambda i: (i, first)), weight, weight]
        + [fixed(b) for b in blocks],
        [shape((wide, n * rows), BF)] * 3,
        [out] * 3,
        (wide // tile,),
        4 * n * rows * width * wide,
        n * rows * wide,
    )


def weight_cols_kernel(n, tiles, at, own, near, *refs):
    xs, outs, x = refs[:n], refs[n : n + tiles], refs[n + tiles]
    rows = xs[0].shape[0]
    half = x.shape[1]

    @pl.when(pl.program_id(0) == 0)
    def _():
        for p in range(n):
            x[p * rows : (p + 1) * rows, :] = lanes(xs[p], at[0], half)[...]

    mid = own.shape[1]
    total = dot_nn(own[...], x[:mid, :]) + dot_nn(near[...], x[mid:, :])
    tile = half // tiles
    for i in range(tiles):
        outs[i][...] = total[:, i * tile : (i + 1) * tile].astype(BF)


def weight_cols(at, xs, own, near, tiles):
    n = len(xs)
    rows, width = xs[0].shape
    half = width // 2
    wide, cols = own.shape
    tile = unit_tile(wide)
    part = pl.BlockSpec((tile, cols), lambda i: (i, 0))
    return call(
        functools.partial(weight_cols_kernel, n, tiles),
        "weight_cols",
        (at, own, near, *xs),
        [SCALARS, part, part] + [fixed(a) for a in xs],
        [shape((wide, half // tiles), BF)] * tiles,
        [pl.BlockSpec((tile, half // tiles), lambda i: (i, 0))] * tiles,
        (wide // tile,),
        2 * n * rows * half * wide,
        scratch=[pltpu.VMEM((n * rows, half), BF)],
    )


def middle_back_kernel(n, at, grad, middle, top, gain, *refs):
    weights, (gm_ref, gb_ref, ga_ref, dg_ref) = refs[:n], refs[n:]
    part = weights[0].shape[0]
    v, dy = middle[...], grad[...]
    scale = scale_of(v)
    dg_ref[...] = jnp.sum(dy * v * scale, 0, keepdims=True)
    a = dy * gain[...]
    gm = top[...].astype(F32) + scale * a - v * (scale**3 * jnp.mean(a * v, -1, keepdims=True))
    gm_ref[...] = gm
    gb = gm.astype(BF)
    gb_ref[...] = gb
    for p in range(n):
        lanes(ga_ref, at[2 + p], part)[...] = dot_nt(gb, weights[p][...]).astype(BF)


def grad_kv_kernel(recv, table, out):
    n_ctx, seq, _, toks, _ = recv.shape
    for k in range(KV_HEADS):
        for s in range(seq):
            total = recv[0, s, k].astype(F32)
            for c in range(1, n_ctx):
                total = total + recv[c, s, k].astype(F32)
            at = slice(s * toks, (s + 1) * toks)
            out[at, k * HEAD : (k + 1) * HEAD] = turn(total[:, :HEAD], table[...], -1.0).astype(BF)
            out[at, (KV_HEADS + k) * HEAD : (KV_HEADS + k + 1) * HEAD] = total[:, HEAD:].astype(BF)


def input_back_kernel(n, at, gq, gkv, tok, gain, gm, *refs):
    wq, wkv, (gi_ref, dg_ref, db_ref, dy_ref) = refs[:n], refs[n : 2 * n], refs[2 * n :]
    part = wq[0].shape[0]
    width = gq.shape[1]
    for p in range(n):
        lanes(dy_ref, at[2 + p], part)[...] = dot_nt(gq[...], wq[p][...]) + dot_nt(
            gkv[...], wkv[p][...]
        )
    db_ref[:, :width] = jnp.sum(gq[...].astype(F32), 0, keepdims=True)
    db_ref[:, width:] = jnp.sum(gkv[...].astype(F32), 0, keepdims=True)
    v, dy = tok[...].astype(F32), dy_ref[...]
    scale = scale_of(v)
    dg_ref[...] = jnp.sum(dy * v * scale, 0, keepdims=True)
    a = dy * gain[...]
    gi_ref[...] = gm[...] + scale * a - v * (scale**3 * jnp.mean(a * v, -1, keepdims=True))


def split_weight_kernel(n, at, *refs):
    xs, gs, (keep, send) = refs[:n], refs[n : 2 * n], refs[2 * n :]
    half = keep.shape[1]
    for out, which in ((keep, at[0]), (send, 1 - at[0])):
        total = dot_tn(xs[0][...], lanes(gs[0], which, half)[...])
        for p in range(1, n):
            total = total + dot_tn(xs[p][...], lanes(gs[p], which, half)[...])
        out[...] = total.astype(out.dtype)


def split_weight(at, xs, gs):
    part, wide = xs[0].shape[1], gs[0].shape[1]
    args = (at, *xs, *gs)
    return call(
        functools.partial(split_weight_kernel, len(xs)),
        "split_weight",
        args,
        [SCALARS] + [whole(a) for a in args[1:]],
        [shape((part, wide // 2), F32), shape((part, wide // 2), BF)],
        flops=2 * len(xs) * xs[0].shape[0] * part * wide,
    )


def join_kernel(tiles, at, *refs):
    mine, theirs, out = refs[:tiles], refs[tiles : 2 * tiles], refs[2 * tiles]
    tile = mine[0].shape[1]
    for j in range(2 * tiles):
        for side, ref in ((0, mine), (1, theirs)):

            @pl.when((at[0] ^ side) == j // tiles)
            def _():
                out[:, j * tile : (j + 1) * tile] = ref[j % tiles][...].astype(F32)


def join(at, mine, theirs):
    tiles = len(mine)
    wide, cols = mine[0].shape
    tile = unit_tile(wide)
    part = pl.BlockSpec((tile, cols), lambda i: (i, 0))
    return call(
        functools.partial(join_kernel, tiles),
        "join",
        (at, *mine, *theirs),
        [SCALARS] + [part] * (2 * tiles),
        [shape((wide, 2 * tiles * cols), F32)],
        [pl.BlockSpec((tile, 2 * tiles * cols), lambda i: (i, 0))],
        (wide // tile,),
    )[0]


def swap(value, axis, offset):
    size = lax.axis_size(axis)
    return lax.ppermute(value, axis, [(i, i ^ offset) for i in range(size)])


def offsets_of(size):
    order = [0]
    step = size // 2
    while step:
        order += [o ^ step for o in order]
        step //= 2
    return order


def gather_dp(value):
    blocks = [value]
    step = lax.axis_size("dp") // 2
    while step:
        blocks += [swap(b, "dp", step) for b in blocks]
        step //= 2
    return blocks


def exchange_dp(value, part):
    here = lax.axis_index("dp")
    out = [lax.dynamic_slice_in_dim(value, here * part, part, 1)]
    for offset in offsets_of(lax.axis_size("dp"))[1:]:
        theirs = lax.dynamic_slice_in_dim(value, (here ^ offset) * part, part, 1)
        out.append(swap(theirs, "dp", offset))
    return out


def scatter_dp(value):
    size = lax.axis_size("dp")
    step = 1
    while step < size:
        half = value.shape[0] // 2
        value = value[:half].astype(F32) + swap(value[half:].astype(BF), "dp", step).astype(F32)
        step *= 2
    return value


def ctx_sums(blocks):
    length = lax.axis_size("ctx") // 2
    last = length - 1
    place = lax.axis_index("ctx") // 2
    depth = length // 2 - 1

    def send(value, pairs):
        return lax.ppermute(
            value, "ctx", [(2 * i + y, 2 * j + y) for i, j in pairs for y in range(2)]
        )

    n = len(blocks)
    state = list(blocks)
    other = [None] * n
    before = []
    n_stage = 2 * depth + 2
    for slot in range(n + n_stage - 1):
        moves = []
        for j in range(depth):
            going, coming = slot - j, slot - (2 * depth - j)
            has_in, has_out = 0 <= going < n, 0 <= coming < n
            inward = [(j, j + 1), (last - j, last - j - 1)]
            outward = [(b, a) for a, b in inward]
            outer = (place == j) | (place == last - j)
            if has_in and has_out and state[going].shape == state[coming].shape:
                value = jnp.where(outer, state[going], state[coming])
                moves.append((value, inward + outward, going, coming, outer))
                continue
            if has_in:
                moves.append((state[going], inward, going, None, outer))
            if has_out:
                moves.append((state[coming], outward, None, coming, outer))
        if 0 <= slot - depth < n:
            b = slot - depth
            moves.append((state[b], [(depth, depth + 1), (depth + 1, depth)], b, None, None))
        if 0 <= slot - n_stage + 1 < n:
            moves.append((state[slot - n_stage + 1], None, None, None, None))
        sent, _ = lax.optimization_barrier(([m[0] for m in moves], before))
        before = []
        for value, (_, pairs, going, coming, outer) in zip(sent, moves):
            got = swap(value, "ctx", 1) if pairs is None else send(value, pairs)
            before.append(got)
            if pairs is None:
                other[slot - n_stage + 1] = got
            if going is not None:
                state[going] = (state[going].astype(F32) + got.astype(F32)).astype(BF)
            if coming is not None:
                state[coming] = jnp.where(outer, got, state[coming])
    return state, other


def shards(
    tokens,
    block_pair,
    gain_attn,
    w_query,
    b_query,
    w_key,
    b_key,
    w_value,
    b_value,
    w_out,
    gain_mlp,
    w_gate,
    w_up,
    w_down,
    cotangent,
):
    n_ctx = lax.axis_size("ctx")
    n_dp = lax.axis_size("dp")
    dp_index = lax.axis_index("dp")
    parity = lax.axis_index("ctx") % 2
    seq_grp, seq_tok, width = tokens.shape
    kv_width = KV_HEADS * HEAD
    rows = seq_grp * seq_tok
    part = w_query.shape[0]
    key_pos = block_positions(block_pair, n_ctx, seq_tok)
    query_pos = lax.dynamic_slice_in_dim(key_pos, lax.axis_index("ctx") * seq_tok, seq_tok)
    table = rope_tables(query_pos)
    qpos = query_pos[:, None]
    kpos = key_pos[None, :]
    at = jnp.stack([parity, dp_index] + [dp_index ^ o for o in offsets_of(n_dp)]).astype(jnp.int32)

    small = lax.all_gather(
        jnp.concatenate([gain_attn, gain_mlp, b_query, b_key, b_value])[None], "dp", axis=0, tiled=True
    )
    cuts = [0]
    for item in (gain_attn, gain_mlp, b_query, b_key, b_value):
        cuts.append(cuts[-1] + item.shape[0])
    gain_one, gain_two, bias_query, bias_key, bias_value = [
        small[:, a:b].reshape(1, -1).astype(F32) for a, b in zip(cuts[:-1], cuts[1:])
    ]
    bias_kv = jnp.concatenate([bias_key, bias_value], 1)
    full_kv = gather_dp(jnp.concatenate([w_key, w_value], 1))
    full_query = gather_dp(w_query)
    full_out = gather_dp(w_out)

    inputs = tokens.reshape(rows, width)
    args = (at, inputs, gain_one, bias_kv, table, *full_kv)
    normed_one, kv_own = call(
        functools.partial(norm_kv_kernel, n_dp, seq_grp),
        "norm_kv",
        args,
        [SCALARS] + [whole(a) for a in args[1:]],
        [shape((rows, width), BF), shape((seq_grp, KV_HEADS, seq_tok, 2 * HEAD), BF)],
        flops=4 * rows * width * kv_width,
    )
    kv_all = lax.all_gather(kv_own, "ctx", axis=0, tiled=False)
    args = (at, normed_one, bias_query, table, *full_query)
    queries = call(
        functools.partial(query_kernel, n_dp),
        "query",
        args,
        [SCALARS] + [whole(a) for a in args[1:]],
        [shape((rows, width), BF)],
        flops=2 * rows * width * width,
    )[0]
    attn_vec = attend_forward(queries, kv_all, qpos, kpos)
    args = (at, inputs, attn_vec, gain_two, *full_out)
    middle, normed_two = call(
        functools.partial(out_norm_kernel, n_dp),
        "out_norm",
        args,
        [SCALARS] + [whole(a) for a in args[1:]],
        [shape((rows, width), F32), shape((rows, width), BF)],
        flops=2 * rows * width * width,
    )

    grad_rows = cotangent.reshape(rows, width)
    top_own, top_near = gather_dp(grad_rows), gather_dp(swap(grad_rows, "ctx", 1))
    norm_own, norm_near = gather_dp(normed_two), gather_dp(swap(normed_two, "ctx", 1))
    wide_gate, wide_up = w_gate.T, w_up.T
    grad_hidden = hidden_back(w_down, top_own + top_near)
    hidden, grad_gate, grad_up = units(grad_hidden, 0, wide_gate, wide_up, norm_own)
    near = units(grad_hidden, 1, wide_gate, wide_up, norm_near)
    tiles = 3
    part_down = weight_cols(at, top_own + top_near, hidden, near[0], tiles)
    part_gate = weight_cols(at, norm_own + norm_near, grad_gate, near[1], tiles)
    part_up = weight_cols(at, norm_own + norm_near, grad_up, near[2], tiles)

    grad_norm_two = scatter_dp(
        (matmul(grad_gate, wide_gate, 0, 0) + matmul(grad_up, wide_up, 0, 0)).astype(BF)
    )
    mlp_out = scatter_dp(matmul(hidden, w_down, 0, 0).astype(BF))
    layer_out = (middle + mlp_out).astype(BF).reshape(tokens.shape)

    args = (at, grad_norm_two, middle, grad_rows, gain_two, *full_out)
    grad_middle, grad_branch, grad_attn, grad_gain_m = call(
        functools.partial(middle_back_kernel, n_dp),
        "middle_back",
        args,
        [SCALARS] + [whole(a) for a in args[1:]],
        [
            shape((rows, width), F32),
            shape((rows, width), BF),
            shape((rows, width), BF),
            shape((1, width), F32),
        ],
        flops=2 * rows * width * width,
    )
    grad_query, grad_kv_all = attend_backward(queries, kv_all, grad_attn, qpos, kpos, table)
    recv = lax.all_to_all(grad_kv_all, "ctx", 0, 0, tiled=True)
    grad_kv = call(
        grad_kv_kernel,
        "grad_kv",
        (recv, table),
        [whole(recv), whole(table)],
        [shape((rows, 2 * kv_width), BF)],
    )[0]
    args = (at, grad_query, grad_kv, inputs, gain_one, grad_middle, *full_query, *full_kv)
    grad_input, grad_gain_a, grad_bias = call(
        functools.partial(input_back_kernel, n_dp),
        "input_back",
        args,
        [SCALARS] + [whole(a) for a in args[1:]],
        [shape((rows, width), F32), shape((1, width), F32), shape((1, width + 2 * kv_width), F32)],
        flops=2 * rows * width * (width + 2 * kv_width),
        scratch=[pltpu.VMEM((rows, width), F32)],
    )

    normed_cols = exchange_dp(normed_one, part)
    attn_cols = exchange_dp(attn_vec, part)
    halves = [
        split_weight(at, attn_cols, gather_dp(grad_branch)),
        split_weight(at, normed_cols, gather_dp(grad_query)),
        split_weight(at, normed_cols, gather_dp(grad_kv)),
    ]
    paired = [(keep + swap(send, "ctx", 1).astype(F32)).astype(BF) for keep, send in halves]

    own, other = ctx_sums(list(part_down) + list(part_gate) + list(part_up) + paired)
    grad_w_down = join(at, own[:tiles], other[:tiles])
    grad_w_gate = join(at, own[tiles : 2 * tiles], other[tiles : 2 * tiles]).T
    grad_w_up = join(at, own[2 * tiles : 3 * tiles], other[2 * tiles : 3 * tiles]).T

    def joined(index):
        mine, theirs = own[index].astype(F32), other[index].astype(F32)
        low = jnp.where(parity == 0, mine, theirs)
        high = jnp.where(parity == 0, theirs, mine)
        return jnp.concatenate([low, high], 1)

    grad_w_out, grad_w_query, grad_w_kv = [joined(3 * tiles + i) for i in range(3)]

    vectors = [
        v.reshape(n_dp, -1)
        for v in (
            grad_gain_a,
            grad_gain_m,
            grad_bias[:, :width],
            grad_bias[:, width : width + kv_width],
            grad_bias[:, width + kv_width :],
        )
    ]
    vectors = jnp.concatenate(vectors, 1)
    order = [lax.dynamic_slice_in_dim(vectors, at[2 + p], 1, 0) for p in range(n_dp)]
    step = 1
    while step < n_dp:
        keep, send = order[: len(order) // 2], order[len(order) // 2 :]
        got = swap(jnp.concatenate(send, 0), "dp", step)
        order = [k + got[i : i + 1] for i, k in enumerate(keep)]
        step *= 2
    share = order[0]
    step = 1
    while step < n_ctx:
        share = share + swap(share, "ctx", step)
        step *= 2
    shares = [share[0, a:b] for a, b in zip(cuts[:-1], cuts[1:])]
    return (
        layer_out,
        grad_input.reshape(tokens.shape),
        shares[0],
        grad_w_query,
        shares[2],
        grad_w_kv[:, :kv_width],
        shares[3],
        grad_w_kv[:, kv_width:],
        shares[4],
        grad_w_out,
        shares[1],
        grad_w_gate,
        grad_w_up,
        grad_w_down,
    )


def solution(mesh):
    placed = (
        P("dp", "ctx", None),
        P(),
        P("dp"),
        P("dp", None),
        P("dp"),
        P("dp", None),
        P("dp"),
        P("dp", None),
        P("dp"),
        P("dp", None),
        P("dp"),
        P(None, "dp"),
        P(None, "dp"),
        P("dp", None),
        P("dp", "ctx", None),
    )
    return jax.shard_map(
        shards,
        mesh=mesh,
        in_specs=placed,
        out_specs=(
            P("dp", "ctx", None),
            P("dp", "ctx", None),
            P("dp"),
            P("dp", None),
            P("dp"),
            P("dp", None),
            P("dp"),
            P("dp", None),
            P("dp"),
            P("dp", None),
            P("dp"),
            P(None, "dp"),
            P(None, "dp"),
            P("dp", None),
        ),
        check_vma=False,
    )
```

```python
import functools
import math

import jax
import jax.numpy as jnp
from jax import lax
from jax.experimental import pallas as pl
from jax.experimental.pallas import tpu as pltpu
from jax.sharding import PartitionSpec as P

HEADS = 12
KV_HEADS = 2
HEAD = 128
GROUP = HEADS // KV_HEADS

EPSILON = 1e-06
THETA = 1000000.0
BF = jnp.bfloat16
F32 = jnp.float32


def matmul(left, right, left_dim, right_dim):
    return lax.dot_general(
        left, right, (((left_dim,), (right_dim,)), ((), ())), preferred_element_type=F32
    )


def dot_nt(left, right):
    return matmul(left, right, 1, 1)


def dot_tn(left, right):
    return matmul(left, right, 0, 0)


def dot_nn(left, right):
    return matmul(left, right, 1, 0)


def block_positions(block_pair, n_ctx, seq_tok):
    half_blk = seq_tok // 2
    row_ids = jnp.arange(n_ctx * seq_tok, dtype=jnp.int32)
    owner = row_ids // seq_tok
    within = row_ids % seq_tok
    matches = owner[:, None] == jnp.arange(n_ctx, dtype=jnp.int32)[None, :]
    first = jnp.sum(jnp.where(matches, block_pair[None, :], 0), 1)
    chosen = jnp.where(within < half_blk, first, 2 * n_ctx - 1 - first)
    return chosen * half_blk + within % half_blk


def rope_tables(positions):
    half_size = HEAD // 2
    freqs = jnp.exp(jnp.arange(half_size, dtype=F32) * (-math.log(THETA) / half_size))
    angle = positions.astype(F32)[:, None] * freqs[None, :]
    cosine, sine = jnp.cos(angle), jnp.sin(angle)
    return jnp.concatenate([cosine, cosine, -sine, sine], 1)


def call(kernel, name, args, specs, outs, out_specs=None, grid=(), flops=0, exps=0, scratch=()):
    size = sum(math.prod(a.shape) * a.dtype.itemsize for a in list(args) + list(outs))
    if out_specs is None:
        out_specs = [whole(o) for o in outs]
    return pl.pallas_call(
        kernel,
        grid=grid,
        in_specs=specs,
        out_specs=out_specs,
        out_shape=outs,
        scratch_shapes=scratch,
        cost_estimate=pl.CostEstimate(flops=flops, transcendentals=exps, bytes_accessed=size),
        name=name,
    )(*args)


SCALARS = pl.BlockSpec(memory_space=pltpu.SMEM)


def whole(array):
    zeros = (0,) * len(array.shape)
    return pl.BlockSpec(array.shape, lambda *_: zeros)


def fixed(array):
    zeros = (0,) * len(array.shape)
    return pl.BlockSpec(array.shape, lambda *_: zeros, pipeline_mode=pl.Buffered(1))


def shape(dims, dtype):
    return jax.ShapeDtypeStruct(tuple(dims), dtype)


def lanes(ref, start, size):
    return ref.at[:, pl.ds(pl.multiple_of(start * size, 128), size)]


def scale_of(x):
    return lax.rsqrt(jnp.mean(x * x, -1, keepdims=True) + EPSILON)


def turn(x, table, sign):
    tables = jnp.concatenate([table] * (x.shape[0] // table.shape[0]), 0)
    return x * tables[:, :HEAD] + sign * (pltpu.roll(x, HEAD // 2, 1) * tables[:, HEAD:])


def norm_kv_kernel(n, seq, at, tok, gain, bias, table, *refs):
    weights, (normed, kv) = refs[:n], refs[n:]
    x = tok[...].astype(F32)
    normed[...] = (x * scale_of(x) * gain[...]).astype(BF)
    part = weights[0].shape[0]
    acc = bias[...]
    for p in range(n):
        acc = acc + dot_nn(lanes(normed, at[2 + p], part)[...], weights[p][...])
    toks = x.shape[0] // seq
    for k in range(KV_HEADS):
        key = turn(acc[:, k * HEAD : (k + 1) * HEAD], table[...], 1.0).astype(BF)
        value = acc[:, (KV_HEADS + k) * HEAD : (KV_HEADS + k + 1) * HEAD].astype(BF)
        for s in range(seq):
            kv[s, k, :, :HEAD] = key[s * toks : (s + 1) * toks]
            kv[s, k, :, HEAD:] = value[s * toks : (s + 1) * toks]


def query_kernel(n, at, normed, bias, table, *refs):
    weights, (out,) = refs[:n], refs[n:]
    part = weights[0].shape[0]
    acc = bias[...]
    for p in range(n):
        acc = acc + dot_nn(lanes(normed, at[2 + p], part)[...], weights[p][...])
    for h in range(HEADS):
        cols = slice(h * HEAD, (h + 1) * HEAD)
        out[:, cols] = turn(acc[:, cols], table[...], 1.0).astype(BF)


def stack_heads(ref):
    return jnp.concatenate([ref[:, g * HEAD : (g + 1) * HEAD] for g in range(GROUP)], 0)


def softmax_of(q, k, qpos, kpos):
    scores = dot_nt(q, k) * (HEAD**-0.5)
    allowed = kpos <= jnp.concatenate([qpos] * GROUP, 0)
    scores = jnp.where(allowed, scores, -jnp.inf)
    expon = jnp.exp(scores - jnp.max(scores, -1, keepdims=True))
    return expon / jnp.sum(expon, -1, keepdims=True)


def attend_forward_kernel(q_ref, kv_ref, qpos, kpos, out_ref):
    rows = q_ref.shape[0]
    keys = kv_ref.shape[0] * kv_ref.shape[1]
    k = kv_ref[:, :, :HEAD].reshape(keys, HEAD)
    v = kv_ref[:, :, HEAD:].reshape(keys, HEAD)
    probs = softmax_of(stack_heads(q_ref), k, qpos[...], kpos[...]).astype(BF)
    mixed = dot_nn(probs, v).astype(BF)
    for g in range(GROUP):
        out_ref[:, g * HEAD : (g + 1) * HEAD] = mixed[g * rows : (g + 1) * rows]


def attention_specs(kv_all):
    n_ctx, _, _, seq_tok, _ = kv_all.shape
    rows = pl.BlockSpec((seq_tok, GROUP * HEAD), lambda s, k: (s, k))
    kv = pl.BlockSpec((n_ctx, None, None, seq_tok, 2 * HEAD), lambda s, k: (0, s, k, 0, 0))
    return rows, kv


def attend_forward(queries, kv_all, qpos, kpos):
    rows, kv = attention_specs(kv_all)
    keys = kv_all.shape[0] * kv_all.shape[3]
    return call(
        attend_forward_kernel,
        "attend_forward",
        (queries, kv_all, qpos, kpos),
        [rows, kv, whole(qpos), whole(kpos)],
        [shape(queries.shape, BF)],
        [rows],
        (kv_all.shape[1], KV_HEADS),
        4 * queries.size * keys,
        queries.shape[0] * HEADS * keys,
    )[0]


def attend_backward_kernel(q_ref, kv_ref, go_ref, qpos, kpos, table, gq_ref, gkv_ref):
    rows = q_ref.shape[0]
    n_ctx, seq_tok, _ = kv_ref.shape
    keys = n_ctx * seq_tok
    scale = HEAD**-0.5
    k = kv_ref[:, :, :HEAD].reshape(keys, HEAD)
    v = kv_ref[:, :, HEAD:].reshape(keys, HEAD)
    q = stack_heads(q_ref)
    go = stack_heads(go_ref)
    probs = softmax_of(q, k, qpos[...], kpos[...])
    gkv_ref[:, :, HEAD:] = dot_tn(probs.astype(BF), go).astype(BF).reshape(n_ctx, seq_tok, HEAD)
    grad_probs = dot_nt(go, v)
    centre = jnp.sum(probs * grad_probs, -1, keepdims=True)
    grad_scores = (probs * (grad_probs - centre)).astype(BF)
    gq = turn(dot_nn(grad_scores, k) * scale, table[...], -1.0).astype(BF)
    for g in range(GROUP):
        gq_ref[:, g * HEAD : (g + 1) * HEAD] = gq[g * rows : (g + 1) * rows]
    gk = dot_tn(grad_scores, q) * scale
    gkv_ref[:, :, :HEAD] = gk.astype(BF).reshape(n_ctx, seq_tok, HEAD)


def attend_backward(queries, kv_all, grad_mixed, qpos, kpos, table):
    rows, kv = attention_specs(kv_all)
    keys = kv_all.shape[0] * kv_all.shape[3]
    return call(
        attend_backward_kernel,
        "attend_backward",
        (queries, kv_all, grad_mixed, qpos, kpos, table),
        [rows, kv, rows, whole(qpos), whole(kpos), whole(table)],
        [shape(queries.shape, BF), shape(kv_all.shape, BF)],
        [rows, kv],
        (kv_all.shape[1], KV_HEADS),
        10 * queries.size * keys,
        queries.shape[0] * HEADS * keys,
    )


def out_norm_kernel(n, at, tok, attn, gain, *refs):
    weights, (middle, normed) = refs[:n], refs[n:]
    part = weights[0].shape[0]
    acc = tok[...].astype(F32)
    for p in range(n):
        acc = acc + dot_nn(lanes(attn, at[2 + p], part)[...], weights[p][...])
    middle[...] = acc
    normed[...] = (acc * scale_of(acc) * gain[...]).astype(BF)


def hidden_back_kernel(n, wd, *refs):
    rows, out = refs[:n], refs[n]
    step = rows[0].shape[0]
    for p in range(n):
        out[:, p * step : (p + 1) * step] = dot_nt(wd[...], rows[p][...]).astype(BF)


def unit_tile(total):
    return max(t for t in range(16, 513, 16) if total % t == 0)


def hidden_back(w_down, blocks):
    n = len(blocks)
    rows, width = blocks[0].shape
    wide = w_down.shape[0]
    tile = unit_tile(wide)
    return call(
        functools.partial(hidden_back_kernel, n),
        "hidden_back",
        (w_down, *blocks),
        [pl.BlockSpec((tile, width), lambda i: (i, 0))] + [fixed(b) for b in blocks],
        [shape((wide, n * rows), BF)],
        [pl.BlockSpec((tile, n * rows), lambda i: (i, 0))],
        (wide // tile,),
        2 * n * rows * width * wide,
    )[0]


def units_kernel(n, gh, wg, wu, *refs):
    rows, (hidden, gg, gu) = refs[:n], refs[n:]
    step = rows[0].shape[0]
    for p in range(n):
        cols = slice(p * step, (p + 1) * step)
        gate = dot_nt(wg[...], rows[p][...])
        up = dot_nt(wu[...], rows[p][...])
        grad = gh[:, cols].astype(F32)
        sigma = 1.0 / (1.0 + jnp.exp(-gate))
        act = gate * sigma
        hidden[:, cols] = (act * up).astype(BF)
        gu[:, cols] = (grad * act).astype(BF)
        gg[:, cols] = (grad * up * sigma * (1.0 + gate - act)).astype(BF)


def units(grad_hidden, first, w_gate, w_up, blocks):
    n = len(blocks)
    rows, width = blocks[0].shape
    wide = w_gate.shape[0]
    tile = unit_tile(wide)
    weight = pl.BlockSpec((tile, width), lambda i: (i, 0))
    out = pl.BlockSpec((tile, n * rows), lambda i: (i, 0))
    return call(
        functools.partial(units_kernel, n),
        "units",
        (grad_hidden, w_gate, w_up, *blocks),
        [pl.BlockSpec((tile, n * rows), lambda i: (i, first)), weight, weight]
        + [fixed(b) for b in blocks],
        [shape((wide, n * rows), BF)] * 3,
        [out] * 3,
        (wide // tile,),
        4 * n * rows * width * wide,
        n * rows * wide,
    )


def weight_tiles_kernel(n, m, flip, at, *refs):
    hs, xs, outs, x = refs[:m], refs[m : m + n], refs[m + n : -1], refs[-1]
    rows, width = xs[0].shape
    size = x.shape[1]

    @pl.when(pl.program_id(0) == 0)
    def _():
        first = (at[0] ^ flip) * size
        for p in range(n):
            x[p * rows : (p + 1) * rows, :] = xs[p][:, pl.ds(pl.multiple_of(first, 128), size)]

    total, row = 0.0, 0
    for h in hs:
        total = total + dot_nn(h[...], x[row : row + h.shape[1], :])
        row += h.shape[1]
    total = total.astype(BF)
    for i, out in enumerate(outs):

        @pl.when(pl.program_id(0) == i)
        def _():
            out[...] = total


TILES = 4


def weight_tiles(at, xs, hs, flip=0):
    n = len(xs)
    rows, width = xs[0].shape
    wide = hs[0].shape[0]
    tile = wide // TILES
    return call(
        functools.partial(weight_tiles_kernel, n, len(hs), flip),
        "weight_tiles",
        (at, *hs, *xs),
        [SCALARS]
        + [pl.BlockSpec((tile, h.shape[1]), lambda i: (i, 0)) for h in hs]
        + [fixed(a) for a in xs],
        [shape((tile, width // 2), BF)] * TILES,
        None,
        (TILES,),
        n * rows * width * wide,
        scratch=[pltpu.VMEM((n * rows, width // 2), BF)],
    )


def rows_back_kernel(n, *refs):
    hs, ws, (keep, send, acc) = refs[:n], refs[n : 2 * n], refs[2 * n :]
    total = dot_tn(hs[0][...], ws[0][...])
    for h, w in zip(hs[1:], ws[1:]):
        total = total + dot_tn(h[...], w[...])
    first = pl.program_id(0) == 0

    @pl.when(first)
    def _():
        acc[...] = total

    @pl.when(jnp.logical_not(first))
    def _():
        acc[...] = acc[...] + total

    @pl.when(pl.program_id(0) == pl.num_programs(0) - 1)
    def _():
        half = keep.shape[0]
        keep[...] = acc[:half, :]
        send[...] = acc[half:, :].astype(BF)


def rows_back(hs, ws):
    wide, rows = hs[0].shape
    width = ws[0].shape[1]
    tile = unit_tile(wide)
    return call(
        functools.partial(rows_back_kernel, len(hs)),
        "rows_back",
        (*hs, *ws),
        [pl.BlockSpec((tile, rows), lambda i: (i, 0))] * len(hs)
        + [pl.BlockSpec((tile, width), lambda i: (i, 0))] * len(ws),
        [shape((rows // 2, width), F32), shape((rows // 2, width), BF)],
        None,
        (wide // tile,),
        2 * len(hs) * wide * rows * width,
        scratch=[pltpu.VMEM((rows, width), F32)],
    )


def middle_back_kernel(n, at, grad, middle, top, gain, *refs):
    weights, (gm_ref, gb_ref, ga_ref, dg_ref) = refs[:n], refs[n:]
    part = weights[0].shape[0]
    v, dy = middle[...], grad[...]
    scale = scale_of(v)
    dg_ref[...] = jnp.sum(dy * v * scale, 0, keepdims=True)
    a = dy * gain[...]
    gm = top[...].astype(F32) + scale * a - v * (scale**3 * jnp.mean(a * v, -1, keepdims=True))
    gm_ref[...] = gm
    gb = gm.astype(BF)
    gb_ref[...] = gb
    for p in range(n):
        lanes(ga_ref, at[2 + p], part)[...] = dot_nt(gb, weights[p][...]).astype(BF)


def grad_kv_kernel(recv, table, out):
    seq, _, toks, _ = recv.shape
    for k in range(KV_HEADS):
        for s in range(seq):
            total = recv[s, k].astype(F32)
            at = slice(s * toks, (s + 1) * toks)
            out[at, k * HEAD : (k + 1) * HEAD] = turn(total[:, :HEAD], table[...], -1.0).astype(BF)
            out[at, (KV_HEADS + k) * HEAD : (KV_HEADS + k + 1) * HEAD] = total[:, HEAD:].astype(BF)


def input_back_kernel(n, at, gq, gkv, tok, gain, gm, *refs):
    wq, wkv, (gi_ref, dg_ref, db_ref, dy_ref) = refs[:n], refs[n : 2 * n], refs[2 * n :]
    part = wq[0].shape[0]
    width = gq.shape[1]
    for p in range(n):
        lanes(dy_ref, at[2 + p], part)[...] = dot_nt(gq[...], wq[p][...]) + dot_nt(
            gkv[...], wkv[p][...]
        )
    db_ref[:, :width] = jnp.sum(gq[...].astype(F32), 0, keepdims=True)
    db_ref[:, width:] = jnp.sum(gkv[...].astype(F32), 0, keepdims=True)
    v, dy = tok[...].astype(F32), dy_ref[...]
    scale = scale_of(v)
    dg_ref[...] = jnp.sum(dy * v * scale, 0, keepdims=True)
    a = dy * gain[...]
    gi_ref[...] = gm[...] + scale * a - v * (scale**3 * jnp.mean(a * v, -1, keepdims=True))


def attention_weights_kernel(n_out, n_query, at, attn, normed, *refs):
    branches, queries, kvs = refs[:n_out], refs[n_out : n_out + n_query], refs[n_out + n_query : -4]

    def product(x, pieces, which, size):
        total, row = 0.0, 0
        for g in pieces:
            total = total + dot_tn(x[row : row + g.shape[0], :], lanes(g, which, size)[...])
            row += g.shape[0]
        return total.astype(BF)

    part, half = attn.shape[1], branches[0].shape[1] // 2
    for outs, which in ((refs[-4:-2], at[0]), (refs[-2:], 1 - at[0])):
        outs[0][:part, :] = product(attn, branches, which, half)
        kv = product(normed, kvs, which, kvs[0].shape[1] // 2)
        cuts = half // kv.shape[1]
        rows = part // cuts
        for j in range(cuts):
            outs[0][part : part + rows, j * kv.shape[1] : (j + 1) * kv.shape[1]] = kv[
                j * rows : (j + 1) * rows
            ]
        outs[0][part + rows :, :] = jnp.zeros((outs[0].shape[0] - part - rows, half), BF)
        outs[1][...] = product(normed, queries, which, half)


def attention_weights(at, rows, attn, normed, branches, queries, kvs):
    part, half = attn.shape[1], branches[0].shape[1] // 2
    args = (at, attn, normed, *branches, *queries, *kvs)
    return call(
        functools.partial(attention_weights_kernel, len(branches), len(queries)),
        "attention_weights",
        args,
        [SCALARS] + [whole(a) for a in args[1:]],
        [shape((rows, half), BF), shape((part, half), BF)] * 2,
        flops=2 * attn.shape[0] * part * 7 * half,
    )


def relay_kernel(flag, fresh, went, arrived, summed, across, sent, go_on, out, done):
    @pl.when(flag[0] == 1)
    def _():
        out[...] = fresh[...]
        done[...] = arrived[...]

    @pl.when(flag[0] == 0)
    def _():
        go_on[...] = (went[...].astype(F32) + arrived[...].astype(F32)).astype(BF)
        out[...] = (summed[...].astype(F32) + across[...].astype(F32)).astype(BF)
        done[...] = sent[...]


def relay(flag, arrays):
    return call(
        relay_kernel,
        "relay",
        (flag, *arrays),
        [SCALARS] + [whole(a) for a in arrays],
        [shape(arrays[0].shape, BF)] * 3,
    )


def join_kernel(at, *refs):
    mine, theirs, out = refs[:TILES], refs[TILES:-1], refs[-1]
    cut = mine[0].shape[1]
    for i in range(TILES):
        for side, tiles in ((0, mine), (1, theirs)):
            for half in range(2):

                @pl.when((pl.program_id(0) == i) & ((at[0] ^ side) == half))
                def _():
                    out[:, half * cut : (half + 1) * cut] = tiles[i][...].astype(F32)


def join(at, mine, theirs):
    rows, cols = mine[0].shape
    return call(
        join_kernel,
        "join",
        (at, *mine, *theirs),
        [SCALARS] + [fixed(a) for a in (*mine, *theirs)],
        [shape((TILES * rows, 2 * cols), F32)],
        [pl.BlockSpec((rows, 2 * cols), lambda i: (i, 0))],
        (TILES,),
    )[0]


def swap(value, axis, offset):
    size = lax.axis_size(axis)
    return lax.ppermute(value, axis, [(i, i ^ offset) for i in range(size)])


def offsets_of(size):
    order = [0]
    step = size // 2
    while step:
        order += [o ^ step for o in order]
        step //= 2
    return order


def tie(values, others):
    return lax.optimization_barrier((values, others))[0]


def swaps(moves, first=(), beside=()):
    sent = tie([m[0] for m in moves], list(first))
    got = [swap(v, *where) for v, (_, *where) in zip(sent, moves)]
    return lax.optimization_barrier((got, list(beside)))[0]


class CtxSums:
    GAP = 2

    def __init__(self, block):
        self.length = lax.axis_size("ctx") // 2
        self.depth = self.length // 2 - 1
        self.place = lax.axis_index("ctx") // 2
        self.number = 0
        self.own, self.other = {}, {}
        self.final = self.own if self.depth != 1 else {}
        self.got, self.arrived = [], []
        ends = (self.place == 0) | (self.place == self.length - 1)
        self.flag = ends.astype(jnp.int32)[None]
        self.sums, self.sends = {}, {}
        self.own[0] = block
        self.moves = self.plan(0)

    def send(self, value, pairs):
        return lax.ppermute(
            value, "ctx", [(2 * i + y, 2 * j + y) for i, j in pairs for y in range(2)]
        )

    def plan(self, now):
        if self.depth == 1:
            return self.short_plan(now)
        last, own = self.length - 1, self.own
        moves = []
        for j in range(self.depth):
            going, coming = now - self.GAP * j, now - self.GAP * (2 * self.depth - j)
            inward = [(j, j + 1), (last - j, last - j - 1)]
            outward = [(b, a) for a, b in inward]
            outer = (self.place == j) | (self.place == last - j)
            if going in own and coming in own:
                value = jnp.where(outer, own[going], own[coming])
                moves.append((value, inward + outward, going, coming, outer))
            elif going in own:
                moves.append((own[going], inward, going, None, outer))
            elif coming in own:
                moves.append((own[coming], outward, None, coming, outer))
        b = now - self.GAP * self.depth
        if b in own:
            across = [(self.depth, self.depth + 1), (self.depth + 1, self.depth)]
            moves.append((own[b], across, b, None, None))
        b = now - self.GAP * (2 * self.depth + 1)
        if b in own:
            moves.append((own[b], None, b, None, None))
        return moves

    def short_plan(self, now):
        own, ends, middle = self.own, [(0, 1), (3, 2)], [(1, 2), (2, 1)]
        entering, leaving = now in own, now - 2 * self.GAP in own
        moves = []
        if entering and not leaving:
            self.sends[now] = own[now]
        if entering or leaving:
            pairs = (ends if entering else []) + ([(b, a) for a, b in ends] if leaving else [])
            moves.append((self.sends[now], pairs, "ends", now, None))
        if now - self.GAP in own:
            moves.append((self.sums[now - self.GAP], middle, "middle", now, None))
        if now - 3 * self.GAP in own:
            b = now - 3 * self.GAP
            moves.append((self.final[b], None, b, None, None))
        return moves

    def short_settle(self):
        now, ends, middle = None, None, None
        for got, (_, pairs, kind, at, _) in self.arrived:
            if pairs is None:
                self.other[kind] = got
                continue
            now = at
            if kind == "ends":
                ends = got
            else:
                middle = got
        self.arrived = []
        if now is None:
            return
        own = self.own
        fresh, went = own.get(now + self.GAP), own.get(now)
        summed, sent = self.sums.get(now - self.GAP), self.sends.get(now)
        if went is not None and middle is None and fresh is not None:
            self.sums[now] = (went.astype(F32) + ends.astype(F32)).astype(BF)
            return
        fill = next(a for a in (ends, middle) if a is not None)
        arrays = [fill if a is None else a for a in (fresh, went, ends, summed, middle, sent)]
        self.sums[now], self.sends[now + self.GAP], self.final[now - 2 * self.GAP] = relay(
            self.flag, arrays
        )

    def settle(self):
        if self.depth == 1:
            return self.short_settle()
        own = self.own
        for got, (_, pairs, going, coming, outer) in self.arrived:
            if pairs is None:
                self.other[going] = got
                continue
            if going is not None:
                own[going] = (own[going].astype(F32) + got.astype(F32)).astype(BF)
            if coming is not None:
                own[coming] = jnp.where(outer, got, own[coming])
        self.arrived = []

    def slot(self, first=(), extra=(), upcoming=None, beside=()):
        now, moves = self.number, self.moves
        self.number += 1
        sent, more = tie(([m[0] for m in moves], [e[0] for e in extra]), (self.got, list(first)))
        got = [
            swap(value, "ctx", 1) if pairs is None else self.send(value, pairs)
            for value, (_, pairs, *_) in zip(sent, moves)
        ]
        got += [swap(value, *where) for value, (_, *where) in zip(more, extra)]
        if upcoming is not None:
            self.own[now + 1] = upcoming()
        self.settle()
        self.moves = self.plan(now + 1)
        got, ready, _ = lax.optimization_barrier((got, [m[0] for m in self.moves], list(beside)))
        self.moves = [(v, *m[1:]) for v, m in zip(ready, self.moves)]
        self.got = got
        self.arrived = list(zip(got, moves))
        return got[len(moves) :]

    def exchanged(self, block):
        if block in self.other:
            return self.other[block]
        for got, (_, pairs, number, *_) in self.arrived:
            if pairs is None and number == block:
                return got
        return None

    def after(self, values):
        return tie(values, self.got)


def shards(
    tokens,
    block_pair,
    gain_attn,
    w_query,
    b_query,
    w_key,
    b_key,
    w_value,
    b_value,
    w_out,
    gain_mlp,
    w_gate,
    w_up,
    w_down,
    cotangent,
):
    n_ctx = lax.axis_size("ctx")
    n_dp = lax.axis_size("dp")
    dp_index = lax.axis_index("dp")
    parity = lax.axis_index("ctx") % 2
    seq_grp, seq_tok, width = tokens.shape
    kv_width = KV_HEADS * HEAD
    rows = seq_grp * seq_tok
    part = w_query.shape[0]
    key_pos = block_positions(block_pair, n_ctx, seq_tok)
    query_pos = lax.dynamic_slice_in_dim(key_pos, lax.axis_index("ctx") * seq_tok, seq_tok)
    table = rope_tables(query_pos)
    qpos = query_pos[:, None]
    kpos = key_pos[None, :]
    at = jnp.stack([parity, dp_index] + [dp_index ^ o for o in offsets_of(n_dp)]).astype(jnp.int32)

    far, close = n_dp // 2, 1
    cuts = [0]
    for item in (gain_attn, gain_mlp, b_query, b_key, b_value):
        cuts.append(cuts[-1] + item.shape[0])
    small = jnp.concatenate([gain_attn, gain_mlp, b_query, b_key, b_value])[None]
    w_kv = jnp.concatenate([w_key, w_value], 1)
    small_x, kv_x, small_c, kv_c = swaps(
        [(small, "dp", far), (w_kv, "dp", far), (small, "dp", close), (w_kv, "dp", close)]
    )
    small_xc, kv_xc = swaps([(small_x, "dp", close), (kv_x, "dp", close)])
    full_kv = [w_kv, kv_x, kv_c, kv_xc]
    gathered = jnp.concatenate([small, small_x, small_c, small_xc], 0).astype(F32)
    picks = at[2:][None, :] == jnp.arange(n_dp, dtype=jnp.int32)[:, None]
    gathered = jnp.sum(jnp.where(picks[:, :, None], gathered[None], 0.0), 1)
    gain_one, gain_two, bias_query, bias_key, bias_value = [
        gathered[:, a:b].reshape(1, -1) for a, b in zip(cuts[:-1], cuts[1:])
    ]
    bias_kv = jnp.concatenate([bias_key, bias_value], 1)

    turn_of = lax.axis_index("ctx") // 2 % 2
    grad_rows = cotangent.reshape(rows, width)
    half_query = lax.dynamic_slice_in_dim(w_query, turn_of * (width // 2), width // 2, 1)
    half_x, top_y, query_c = swaps(
        [(half_query, "dp", far), (grad_rows, "ctx", 1), (w_query, "dp", close)], [kv_x]
    )

    inputs = tokens.reshape(rows, width)
    args = (at, inputs, gain_one, bias_kv, table, *full_kv)
    normed_one, kv_own = call(
        functools.partial(norm_kv_kernel, n_dp, seq_grp),
        "norm_kv",
        args,
        [SCALARS] + [whole(a) for a in args[1:]],
        [shape((rows, width), BF), shape((seq_grp, KV_HEADS, seq_tok, 2 * HEAD), BF)],
        flops=4 * rows * width * kv_width,
    )
    kv_all = lax.all_gather(kv_own, "ctx", axis=0, tiled=False)
    half_z, top_x = swaps([(half_x, "ctx", 2), (grad_rows, "dp", far)], [half_x])
    query_x = jnp.concatenate(
        [jnp.where(turn_of == 0, half_x, half_z), jnp.where(turn_of == 0, half_z, half_x)], 1
    )
    (query_xc,) = swaps([(query_x, "dp", close)])
    full_query = [w_query, query_x, query_c, query_xc]
    args = (at, normed_one, bias_query, table, *full_query)
    queries = call(
        functools.partial(query_kernel, n_dp),
        "query",
        args,
        [SCALARS] + [whole(a) for a in args[1:]],
        [shape((rows, width), BF)],
        flops=2 * rows * width * width,
    )[0]
    out_x, out_c, top_xy, top_c = swaps(
        [(w_out, "dp", far), (w_out, "dp", close), (top_x, "ctx", 1), (grad_rows, "dp", close)],
        [top_x],
        [queries],
    )
    attn_vec = attend_forward(queries, kv_all, qpos, kpos)
    out_xc, top_xc, top_yc, top_xyc = swaps(
        [(out_x, "dp", close), (top_x, "dp", close), (top_y, "dp", close), (top_xy, "dp", close)],
        [out_x],
        [attn_vec],
    )
    full_out = [w_out, out_x, out_c, out_xc]
    tops = [grad_rows, top_x, top_c, top_xc, top_y, top_xy, top_yc, top_xyc]
    args = (at, inputs, attn_vec, gain_two, *full_out)
    middle, normed_two = call(
        functools.partial(out_norm_kernel, n_dp),
        "out_norm",
        args,
        [SCALARS] + [whole(a) for a in args[1:]],
        [shape((rows, width), F32), shape((rows, width), BF)],
        flops=2 * rows * width * width,
    )

    tops = tie(tops, normed_two)
    grad_hidden = hidden_back(w_down, tops)
    norm_x, norm_y, norm_c = swaps(
        [(normed_two, "dp", far), (normed_two, "ctx", 1), (normed_two, "dp", close)],
        [],
        [grad_hidden],
    )
    (norm_xc,) = swaps([(norm_x, "dp", close)])
    wide_gate, wide_up = w_gate.T, w_up.T
    norm_own = [normed_two, norm_x, norm_c, norm_xc]
    hidden, grad_gate, grad_up = units(grad_hidden, 0, wide_gate, wide_up, norm_own)
    norm_yx, norm_yc = swaps(
        [(norm_y, "dp", far), (norm_y, "dp", close)], [norm_xc], [hidden]
    )
    (norm_yxc,) = swaps([(norm_yx, "dp", close)], [norm_xc], [hidden])
    norms = norm_own + [norm_y, norm_yx, norm_yc, norm_yxc]
    peers = offsets_of(n_dp)[1:]

    def columns(value):
        return [
            (lax.dynamic_slice_in_dim(value, (dp_index ^ o) * part, part, 1), "dp", o) for o in peers
        ]

    def with_own(value, got):
        return jnp.concatenate(
            [lax.dynamic_slice_in_dim(value, dp_index * part, part, 1)] + list(got), 0
        )

    near = units(grad_hidden, 1, wide_gate, wide_up, norms[n_dp:])
    down = weight_tiles(at, tops, [hidden, near[0]])
    line = CtxSums(down[0])

    gate_now, up_now = tie((grad_gate, grad_up), down)
    partial, sent = rows_back([gate_now, up_now], [wide_gate, wide_up])
    normed_cols = line.slot(down, columns(normed_one), lambda: down[1], [partial])
    normed_cols = with_own(normed_one, normed_cols)
    gn_got, *attn_cols = line.slot(
        [partial, sent], [(sent, "dp", close)] + columns(attn_vec), lambda: down[2]
    )
    attn_cols = with_own(attn_vec, attn_cols)
    partial = partial + gn_got.astype(F32)
    sent = partial[rows:].astype(BF)
    gate_now, near_now = line.after((grad_gate, near[1]))
    gate = weight_tiles(at, norms, [gate_now, near_now])
    (gn_got,) = line.slot([sent], [(sent, "dp", far)], lambda: down[3])
    grad_norm_two = partial[:rows] + gn_got.astype(F32)

    args = (at, grad_norm_two, middle, grad_rows, gain_two, *full_out)
    grad_middle, grad_branch, grad_attn, grad_gain_m = call(
        functools.partial(middle_back_kernel, n_dp),
        "middle_back",
        args,
        [SCALARS] + [whole(a) for a in args[1:]],
        [
            shape((rows, width), F32),
            shape((rows, width), BF),
            shape((rows, width), BF),
            shape((1, width), F32),
        ],
        flops=2 * rows * width * width,
    )
    grad_query, grad_kv_all = attend_backward(queries, kv_all, grad_attn, qpos, kpos, table)
    recv = lax.psum_scatter(grad_kv_all, "ctx", scatter_dimension=0, tiled=False)
    line.slot(gate, [], lambda: gate[0])
    (branch_x,) = line.slot([grad_query], [(grad_branch, "dp", far)], lambda: gate[1])
    branches = [jnp.concatenate([grad_branch, branch_x], 0)]
    up_now, near_now = line.after((grad_up, near[2]))
    up = weight_tiles(at, norms, [up_now, near_now])
    query_x, got = line.slot(
        branches, [(grad_query, "dp", far), (branches[0], "dp", close)], lambda: gate[2]
    )
    branches.append(got)
    queries_back = [jnp.concatenate([grad_query, query_x], 0)]
    mlp_partial, mlp_sent = rows_back([tie(hidden, (up, line.got))], [w_down])
    (got,) = line.slot(
        [*up, *queries_back], [(queries_back[0], "dp", close)], lambda: gate[3]
    )
    queries_back.append(got)
    grad_kv = call(
        grad_kv_kernel,
        "grad_kv",
        (recv, table),
        [whole(recv), whole(table)],
        [shape((rows, 2 * kv_width), BF)],
    )[0]
    (mlp_got,) = line.slot([mlp_partial, mlp_sent], [(mlp_sent, "dp", close)], lambda: up[0])
    mlp_partial = mlp_partial + mlp_got.astype(F32)
    mlp_sent = mlp_partial[rows:].astype(BF)
    kvs = line.slot([grad_kv], [(grad_kv, "dp", o) for o in peers], lambda: up[1])
    kvs = [grad_kv, *kvs]
    args = (at, grad_query, grad_kv, inputs, gain_one, grad_middle, *full_query, *full_kv)
    grad_input, grad_gain_a, grad_bias = call(
        functools.partial(input_back_kernel, n_dp),
        "input_back",
        args,
        [SCALARS] + [whole(a) for a in args[1:]],
        [shape((rows, width), F32), shape((1, width), F32), shape((1, width + 2 * kv_width), F32)],
        flops=2 * rows * width * (width + 2 * kv_width),
        scratch=[pltpu.VMEM((rows, width), F32)],
    )
    vectors = jnp.concatenate(
        [
            v.reshape(n_dp, -1)
            for v in (
                grad_gain_a,
                grad_gain_m,
                grad_bias[:, :width],
                grad_bias[:, width : width + kv_width],
                grad_bias[:, width + kv_width :],
            )
        ],
        1,
    )
    shares = [lax.dynamic_slice_in_dim(vectors, at[2 + p], 1, 0) for p in range(n_dp)]
    tile_rows = down[0].shape[0]
    out_keep, query_keep, out_send, query_send = attention_weights(
        at, tile_rows, attn_cols, normed_cols, branches, queries_back, kvs
    )
    got = line.slot(
        [grad_input, *shares], [(s, "dp", o) for s, o in zip(shares[1:], peers)], lambda: up[2]
    )
    share = sum(got, shares[0])
    share_half = cuts[-1] // 2

    def with_share(block, which):
        own = lax.dynamic_slice_in_dim(share, which * share_half, share_half, 1).astype(BF)
        below = tile_rows - part
        own = jnp.pad(own, ((0, below - 1), (0, width // 2 - share_half)))
        return jnp.concatenate([block, own], 0)

    query_keep, query_send = with_share(query_keep, parity), with_share(query_send, 1 - parity)
    (got,) = line.slot([out_keep, out_send], [(out_send, "ctx", 1)], lambda: up[3])
    out_block = (out_keep.astype(F32) + got.astype(F32)).astype(BF)

    def sides(first):
        numbers = range(first, first + TILES)
        return [[line.final[i] for i in numbers], [line.exchanged(i) for i in numbers]]

    full = {}

    def join_next():
        first = len(full) * TILES
        if len(full) == 3 or line.exchanged(first + TILES - 1) is None:
            return []
        full[len(full)] = join(at, *line.after(sides(first)))
        return [full[len(full) - 1]]

    joined = join_next()
    (got,) = line.slot([query_keep, query_send], [(query_send, "ctx", 1)], lambda: out_block)
    query_block = (query_keep.astype(F32) + got.astype(F32)).astype(BF)
    (mlp_got,) = line.slot([*joined, mlp_sent], [(mlp_sent, "dp", far)], lambda: query_block)
    layer_out = (line.after(middle) + mlp_partial[:rows] + mlp_got.astype(F32)).astype(BF)
    layer_out = layer_out.reshape(tokens.shape)
    last = 3 * TILES + 1

    def both(block, mine, theirs):
        mine, theirs = mine.astype(F32), theirs.astype(F32)
        return jnp.where(parity == 0, mine, theirs), jnp.where(parity == 0, theirs, mine)

    while last not in line.other:
        beside = [] if line.number != 3 * TILES + 1 else [layer_out]
        beside += join_next()
        if line.moves:
            line.slot(beside=beside)
        else:
            line.settle()
    while len(full) < 3:
        join_next()
    grad_w_down, grad_w_gate, grad_w_up = [full[i] for i in range(3)]
    pairs = [both(b, line.final[b], line.other[b]) for b in (last - 1, last)]
    grad_w_out = jnp.concatenate([p[:part] for p in pairs[0]], 1)
    grad_w_query = jnp.concatenate([p[:part] for p in pairs[1]], 1)
    share = jnp.concatenate([p[part : part + 1, :share_half] for p in pairs[1]], 1)
    pieces = width // 2 // kv_width
    kv_rows = part // pieces
    grad_w_kv = [
        jnp.concatenate(
            [p[part : part + kv_rows, j * kv_width : (j + 1) * kv_width] for j in range(pieces)], 0
        )
        for p in pairs[0]
    ]
    grad_w_kv = jnp.concatenate(grad_w_kv, 1)

    shares = [share[0, a:b] for a, b in zip(cuts[:-1], cuts[1:])]
    return (
        layer_out,
        grad_input.reshape(tokens.shape),
        shares[0],
        grad_w_query,
        shares[2],
        grad_w_kv[:, :kv_width],
        shares[3],
        grad_w_kv[:, kv_width:],
        shares[4],
        grad_w_out,
        shares[1],
        grad_w_gate.T,
        grad_w_up.T,
        grad_w_down,
    )


def solution(mesh):
    placed = (
        P("dp", "ctx", None),
        P(),
        P("dp"),
        P("dp", None),
        P("dp"),
        P("dp", None),
        P("dp"),
        P("dp", None),
        P("dp"),
        P("dp", None),
        P("dp"),
        P(None, "dp"),
        P(None, "dp"),
        P("dp", None),
        P("dp", "ctx", None),
    )
    return jax.shard_map(
        shards,
        mesh=mesh,
        in_specs=placed,
        out_specs=(
            P("dp", "ctx", None),
            P("dp", "ctx", None),
            P("dp"),
            P("dp", None),
            P("dp"),
            P("dp", None),
            P("dp"),
            P("dp", None),
            P("dp"),
            P("dp", None),
            P("dp"),
            P(None, "dp"),
            P(None, "dp"),
            P("dp", None),
        ),
        check_vma=False,
    )
```

```python
import functools
import math

import jax
import jax.numpy as jnp
from jax import lax
from jax.experimental import pallas as pl
from jax.experimental.pallas import tpu as pltpu
from jax.sharding import PartitionSpec as P

HEADS = 12
KV_HEADS = 2
HEAD = 128
GROUP = HEADS // KV_HEADS

EPSILON = 1e-06
THETA = 1000000.0
BF = jnp.bfloat16
F32 = jnp.float32


def matmul(left, right, left_dim, right_dim):
    return lax.dot_general(
        left, right, (((left_dim,), (right_dim,)), ((), ())), preferred_element_type=F32
    )


def dot_nt(left, right):
    return matmul(left, right, 1, 1)


def dot_tn(left, right):
    return matmul(left, right, 0, 0)


def dot_nn(left, right):
    return matmul(left, right, 1, 0)


def block_positions(block_pair, n_ctx, seq_tok):
    half_blk = seq_tok // 2
    row_ids = jnp.arange(n_ctx * seq_tok, dtype=jnp.int32)
    owner = row_ids // seq_tok
    within = row_ids % seq_tok
    matches = owner[:, None] == jnp.arange(n_ctx, dtype=jnp.int32)[None, :]
    first = jnp.sum(jnp.where(matches, block_pair[None, :], 0), 1)
    chosen = jnp.where(within < half_blk, first, 2 * n_ctx - 1 - first)
    return chosen * half_blk + within % half_blk


def rope_tables(positions):
    half_size = HEAD // 2
    freqs = jnp.exp(jnp.arange(half_size, dtype=F32) * (-math.log(THETA) / half_size))
    angle = positions.astype(F32)[:, None] * freqs[None, :]
    cosine, sine = jnp.cos(angle), jnp.sin(angle)
    return jnp.concatenate([cosine, cosine, -sine, sine], 1)


def call(kernel, name, args, specs, outs, out_specs=None, grid=(), flops=0, exps=0, scratch=()):
    size = sum(math.prod(a.shape) * a.dtype.itemsize for a in list(args) + list(outs))
    if out_specs is None:
        out_specs = [whole(o) for o in outs]
    return pl.pallas_call(
        kernel,
        grid=grid,
        in_specs=specs,
        out_specs=out_specs,
        out_shape=outs,
        scratch_shapes=scratch,
        cost_estimate=pl.CostEstimate(flops=flops, transcendentals=exps, bytes_accessed=size),
        name=name,
    )(*args)


SCALARS = pl.BlockSpec(memory_space=pltpu.SMEM)


def whole(array):
    zeros = (0,) * len(array.shape)
    return pl.BlockSpec(array.shape, lambda *_: zeros)


def fixed(array):
    zeros = (0,) * len(array.shape)
    return pl.BlockSpec(array.shape, lambda *_: zeros, pipeline_mode=pl.Buffered(1))


def shape(dims, dtype):
    return jax.ShapeDtypeStruct(tuple(dims), dtype)


def lanes(ref, start, size):
    return ref.at[:, pl.ds(pl.multiple_of(start * size, 128), size)]


def scale_of(x):
    return lax.rsqrt(jnp.mean(x * x, -1, keepdims=True) + EPSILON)


def turn(x, table, sign):
    tables = jnp.concatenate([table] * (x.shape[0] // table.shape[0]), 0)
    return x * tables[:, :HEAD] + sign * (pltpu.roll(x, HEAD // 2, 1) * tables[:, HEAD:])


def norm_kv_kernel(n, seq, at, tok, gain, bias, table, *refs):
    weights, (normed, kv) = refs[:n], refs[n:]
    x = tok[...].astype(F32)
    normed[...] = (x * scale_of(x) * gain[...]).astype(BF)
    part = weights[0].shape[0]
    acc = bias[...]
    for p in range(n):
        acc = acc + dot_nn(lanes(normed, at[2 + p], part)[...], weights[p][...])
    toks = x.shape[0] // seq
    for k in range(KV_HEADS):
        key = turn(acc[:, k * HEAD : (k + 1) * HEAD], table[...], 1.0).astype(BF)
        value = acc[:, (KV_HEADS + k) * HEAD : (KV_HEADS + k + 1) * HEAD].astype(BF)
        for s in range(seq):
            kv[s, k, :, :HEAD] = key[s * toks : (s + 1) * toks]
            kv[s, k, :, HEAD:] = value[s * toks : (s + 1) * toks]


def query_kernel(n, at, normed, bias, table, *refs):
    weights, (out,) = refs[:n], refs[n:]
    part = weights[0].shape[0]
    acc = bias[...]
    for p in range(n):
        acc = acc + dot_nn(lanes(normed, at[2 + p], part)[...], weights[p][...])
    for h in range(HEADS):
        cols = slice(h * HEAD, (h + 1) * HEAD)
        out[:, cols] = turn(acc[:, cols], table[...], 1.0).astype(BF)


def stack_heads(ref):
    return jnp.concatenate([ref[:, g * HEAD : (g + 1) * HEAD] for g in range(GROUP)], 0)


def softmax_of(q, k, qpos, kpos):
    scores = dot_nt(q, k) * (HEAD**-0.5)
    allowed = kpos <= jnp.concatenate([qpos] * GROUP, 0)
    scores = jnp.where(allowed, scores, -jnp.inf)
    expon = jnp.exp(scores - jnp.max(scores, -1, keepdims=True))
    return expon / jnp.sum(expon, -1, keepdims=True)


def attend_forward_kernel(q_ref, kv_ref, qpos, kpos, out_ref):
    rows = q_ref.shape[0]
    keys = kv_ref.shape[0] * kv_ref.shape[1]
    k = kv_ref[:, :, :HEAD].reshape(keys, HEAD)
    v = kv_ref[:, :, HEAD:].reshape(keys, HEAD)
    probs = softmax_of(stack_heads(q_ref), k, qpos[...], kpos[...]).astype(BF)
    mixed = dot_nn(probs, v).astype(BF)
    for g in range(GROUP):
        out_ref[:, g * HEAD : (g + 1) * HEAD] = mixed[g * rows : (g + 1) * rows]


def attention_specs(kv_all):
    n_ctx, _, _, seq_tok, _ = kv_all.shape
    rows = pl.BlockSpec((seq_tok, GROUP * HEAD), lambda s, k: (s, k))
    kv = pl.BlockSpec((n_ctx, None, None, seq_tok, 2 * HEAD), lambda s, k: (0, s, k, 0, 0))
    return rows, kv


def attend_forward(queries, kv_all, qpos, kpos):
    rows, kv = attention_specs(kv_all)
    keys = kv_all.shape[0] * kv_all.shape[3]
    return call(
        attend_forward_kernel,
        "attend_forward",
        (queries, kv_all, qpos, kpos),
        [rows, kv, whole(qpos), whole(kpos)],
        [shape(queries.shape, BF)],
        [rows],
        (kv_all.shape[1], KV_HEADS),
        4 * queries.size * keys,
        queries.shape[0] * HEADS * keys,
    )[0]


def attend_backward_kernel(q_ref, kv_ref, go_ref, qpos, kpos, table, gq_ref, gkv_ref):
    rows = q_ref.shape[0]
    n_ctx, seq_tok, _ = kv_ref.shape
    keys = n_ctx * seq_tok
    scale = HEAD**-0.5
    k = kv_ref[:, :, :HEAD].reshape(keys, HEAD)
    v = kv_ref[:, :, HEAD:].reshape(keys, HEAD)
    q = stack_heads(q_ref)
    go = stack_heads(go_ref)
    probs = softmax_of(q, k, qpos[...], kpos[...])
    gkv_ref[:, :, HEAD:] = dot_tn(probs.astype(BF), go).astype(BF).reshape(n_ctx, seq_tok, HEAD)
    grad_probs = dot_nt(go, v)
    centre = jnp.sum(probs * grad_probs, -1, keepdims=True)
    grad_scores = (probs * (grad_probs - centre)).astype(BF)
    gq = turn(dot_nn(grad_scores, k) * scale, table[...], -1.0).astype(BF)
    for g in range(GROUP):
        gq_ref[:, g * HEAD : (g + 1) * HEAD] = gq[g * rows : (g + 1) * rows]
    gk = dot_tn(grad_scores, q) * scale
    gkv_ref[:, :, :HEAD] = gk.astype(BF).reshape(n_ctx, seq_tok, HEAD)


def attend_backward(queries, kv_all, grad_mixed, qpos, kpos, table):
    rows, kv = attention_specs(kv_all)
    keys = kv_all.shape[0] * kv_all.shape[3]
    return call(
        attend_backward_kernel,
        "attend_backward",
        (queries, kv_all, grad_mixed, qpos, kpos, table),
        [rows, kv, rows, whole(qpos), whole(kpos), whole(table)],
        [shape(queries.shape, BF), shape(kv_all.shape, BF)],
        [rows, kv],
        (kv_all.shape[1], KV_HEADS),
        10 * queries.size * keys,
        queries.shape[0] * HEADS * keys,
    )


def out_norm_kernel(n, at, tok, attn, gain, *refs):
    weights, (middle, normed) = refs[:n], refs[n:]
    part = weights[0].shape[0]
    acc = tok[...].astype(F32)
    for p in range(n):
        acc = acc + dot_nn(lanes(attn, at[2 + p], part)[...], weights[p][...])
    middle[...] = acc
    normed[...] = (acc * scale_of(acc) * gain[...]).astype(BF)


def hidden_back_kernel(n, wd, *refs):
    rows, out = refs[:n], refs[n]
    step = rows[0].shape[0]
    for p in range(n):
        out[:, p * step : (p + 1) * step] = dot_nt(wd[...], rows[p][...]).astype(BF)


def unit_tile(total):
    return max(t for t in range(16, 513, 16) if total % t == 0)


def hidden_back(w_down, blocks):
    n = len(blocks)
    rows, width = blocks[0].shape
    wide = w_down.shape[0]
    tile = unit_tile(wide)
    return call(
        functools.partial(hidden_back_kernel, n),
        "hidden_back",
        (w_down, *blocks),
        [pl.BlockSpec((tile, width), lambda i: (i, 0))] + [fixed(b) for b in blocks],
        [shape((wide, n * rows), BF)],
        [pl.BlockSpec((tile, n * rows), lambda i: (i, 0))],
        (wide // tile,),
        2 * n * rows * width * wide,
    )[0]


def units_kernel(n, gh, wg, wu, *refs):
    rows, (hidden, gg, gu) = refs[:n], refs[n:]
    step = rows[0].shape[0]
    for p in range(n):
        cols = slice(p * step, (p + 1) * step)
        gate = dot_nt(wg[...], rows[p][...])
        up = dot_nt(wu[...], rows[p][...])
        grad = gh[:, cols].astype(F32)
        sigma = 1.0 / (1.0 + jnp.exp(-gate))
        act = gate * sigma
        hidden[:, cols] = (act * up).astype(BF)
        gu[:, cols] = (grad * act).astype(BF)
        gg[:, cols] = (grad * up * sigma * (1.0 + gate - act)).astype(BF)


def units(grad_hidden, first, w_gate, w_up, blocks):
    n = len(blocks)
    rows, width = blocks[0].shape
    wide = w_gate.shape[0]
    tile = unit_tile(wide)
    weight = pl.BlockSpec((tile, width), lambda i: (i, 0))
    out = pl.BlockSpec((tile, n * rows), lambda i: (i, 0))
    return call(
        functools.partial(units_kernel, n),
        "units",
        (grad_hidden, w_gate, w_up, *blocks),
        [pl.BlockSpec((tile, n * rows), lambda i: (i, first)), weight, weight]
        + [fixed(b) for b in blocks],
        [shape((wide, n * rows), BF)] * 3,
        [out] * 3,
        (wide // tile,),
        4 * n * rows * width * wide,
        n * rows * wide,
    )


def weight_tiles_kernel(n, m, flip, at, *refs):
    hs, xs, outs, x = refs[:m], refs[m : m + n], refs[m + n : -1], refs[-1]
    rows, width = xs[0].shape
    size = x.shape[1]

    @pl.when(pl.program_id(0) == 0)
    def _():
        first = (at[0] ^ flip) * size
        for p in range(n):
            x[p * rows : (p + 1) * rows, :] = xs[p][:, pl.ds(pl.multiple_of(first, 128), size)]

    total, row = 0.0, 0
    for h in hs:
        total = total + dot_nn(h[...], x[row : row + h.shape[1], :])
        row += h.shape[1]
    total = total.astype(BF)
    for i, out in enumerate(outs):

        @pl.when(pl.program_id(0) == i)
        def _():
            out[...] = total


TILES = 4


def weight_tiles(at, xs, hs, flip=0):
    n = len(xs)
    rows, width = xs[0].shape
    wide = hs[0].shape[0]
    tile = wide // TILES
    return call(
        functools.partial(weight_tiles_kernel, n, len(hs), flip),
        "weight_tiles",
        (at, *hs, *xs),
        [SCALARS]
        + [pl.BlockSpec((tile, h.shape[1]), lambda i: (i, 0)) for h in hs]
        + [fixed(a) for a in xs],
        [shape((tile, width // 2), BF)] * TILES,
        None,
        (TILES,),
        n * rows * width * wide,
        scratch=[pltpu.VMEM((n * rows, width // 2), BF)],
    )


def rows_back_kernel(n, *refs):
    hs, ws, (keep, send, acc) = refs[:n], refs[n : 2 * n], refs[2 * n :]
    total = dot_tn(hs[0][...], ws[0][...])
    for h, w in zip(hs[1:], ws[1:]):
        total = total + dot_tn(h[...], w[...])
    first = pl.program_id(0) == 0

    @pl.when(first)
    def _():
        acc[...] = total

    @pl.when(jnp.logical_not(first))
    def _():
        acc[...] = acc[...] + total

    @pl.when(pl.program_id(0) == pl.num_programs(0) - 1)
    def _():
        half = keep.shape[0]
        keep[...] = acc[:half, :]
        send[...] = acc[half:, :].astype(BF)


def rows_back(hs, ws):
    wide, rows = hs[0].shape
    width = ws[0].shape[1]
    tile = unit_tile(wide)
    return call(
        functools.partial(rows_back_kernel, len(hs)),
        "rows_back",
        (*hs, *ws),
        [pl.BlockSpec((tile, rows), lambda i: (i, 0))] * len(hs)
        + [pl.BlockSpec((tile, width), lambda i: (i, 0))] * len(ws),
        [shape((rows // 2, width), F32), shape((rows // 2, width), BF)],
        None,
        (wide // tile,),
        2 * len(hs) * wide * rows * width,
        scratch=[pltpu.VMEM((rows, width), F32)],
    )


def middle_back_kernel(n, at, grad, middle, top, gain, *refs):
    weights, (gm_ref, gb_ref, ga_ref, dg_ref) = refs[:n], refs[n:]
    part = weights[0].shape[0]
    v, dy = middle[...], grad[...]
    scale = scale_of(v)
    dg_ref[...] = jnp.sum(dy * v * scale, 0, keepdims=True)
    a = dy * gain[...]
    gm = top[...].astype(F32) + scale * a - v * (scale**3 * jnp.mean(a * v, -1, keepdims=True))
    gm_ref[...] = gm
    gb = gm.astype(BF)
    gb_ref[...] = gb
    for p in range(n):
        lanes(ga_ref, at[2 + p], part)[...] = dot_nt(gb, weights[p][...]).astype(BF)


def grad_kv_kernel(recv, table, out):
    seq, _, toks, _ = recv.shape
    for k in range(KV_HEADS):
        for s in range(seq):
            total = recv[s, k].astype(F32)
            at = slice(s * toks, (s + 1) * toks)
            out[at, k * HEAD : (k + 1) * HEAD] = turn(total[:, :HEAD], table[...], -1.0).astype(BF)
            out[at, (KV_HEADS + k) * HEAD : (KV_HEADS + k + 1) * HEAD] = total[:, HEAD:].astype(BF)


def input_back_kernel(n, at, gq, gkv, tok, gain, gm, *refs):
    wq, wkv, (gi_ref, dg_ref, db_ref, dy_ref) = refs[:n], refs[n : 2 * n], refs[2 * n :]
    part = wq[0].shape[0]
    width = gq.shape[1]
    for p in range(n):
        lanes(dy_ref, at[2 + p], part)[...] = dot_nt(gq[...], wq[p][...]) + dot_nt(
            gkv[...], wkv[p][...]
        )
    db_ref[:, :width] = jnp.sum(gq[...].astype(F32), 0, keepdims=True)
    db_ref[:, width:] = jnp.sum(gkv[...].astype(F32), 0, keepdims=True)
    v, dy = tok[...].astype(F32), dy_ref[...]
    scale = scale_of(v)
    dg_ref[...] = jnp.sum(dy * v * scale, 0, keepdims=True)
    a = dy * gain[...]
    gi_ref[...] = gm[...] + scale * a - v * (scale**3 * jnp.mean(a * v, -1, keepdims=True))


def attention_weights_kernel(n_out, n_query, at, attn, normed, *refs):
    branches, queries, kvs = refs[:n_out], refs[n_out : n_out + n_query], refs[n_out + n_query : -4]

    def product(x, pieces, which, size):
        total, row = 0.0, 0
        for g in pieces:
            total = total + dot_tn(x[row : row + g.shape[0], :], lanes(g, which, size)[...])
            row += g.shape[0]
        return total.astype(BF)

    part, half = attn.shape[1], branches[0].shape[1] // 2
    for outs, which in ((refs[-4:-2], at[0]), (refs[-2:], 1 - at[0])):
        outs[0][:part, :] = product(attn, branches, which, half)
        kv = product(normed, kvs, which, kvs[0].shape[1] // 2)
        cuts = half // kv.shape[1]
        rows = part // cuts
        for j in range(cuts):
            outs[0][part : part + rows, j * kv.shape[1] : (j + 1) * kv.shape[1]] = kv[
                j * rows : (j + 1) * rows
            ]
        outs[0][part + rows :, :] = jnp.zeros((outs[0].shape[0] - part - rows, half), BF)
        outs[1][...] = product(normed, queries, which, half)


def attention_weights(at, rows, attn, normed, branches, queries, kvs):
    part, half = attn.shape[1], branches[0].shape[1] // 2
    args = (at, attn, normed, *branches, *queries, *kvs)
    return call(
        functools.partial(attention_weights_kernel, len(branches), len(queries)),
        "attention_weights",
        args,
        [SCALARS] + [whole(a) for a in args[1:]],
        [shape((rows, half), BF), shape((part, half), BF)] * 2,
        flops=2 * attn.shape[0] * part * 7 * half,
    )


def relay_kernel(flag, fresh, went, arrived, summed, across, sent, go_on, out, done):
    @pl.when(flag[0] == 1)
    def _():
        out[...] = fresh[...]
        done[...] = arrived[...]

    @pl.when(flag[0] == 0)
    def _():
        go_on[...] = (went[...].astype(F32) + arrived[...].astype(F32)).astype(BF)
        out[...] = (summed[...].astype(F32) + across[...].astype(F32)).astype(BF)
        done[...] = sent[...]


def relay(flag, arrays):
    return call(
        relay_kernel,
        "relay",
        (flag, *arrays),
        [SCALARS] + [whole(a) for a in arrays],
        [shape(arrays[0].shape, BF)] * 3,
    )


def join_kernel(at, *refs):
    mine, theirs, out = refs[:TILES], refs[TILES:-1], refs[-1]
    cut = mine[0].shape[1]
    for i in range(TILES):
        for side, tiles in ((0, mine), (1, theirs)):
            for half in range(2):

                @pl.when((pl.program_id(0) == i) & ((at[0] ^ side) == half))
                def _():
                    out[:, half * cut : (half + 1) * cut] = tiles[i][...].astype(F32)


def join(at, mine, theirs):
    rows, cols = mine[0].shape
    return call(
        join_kernel,
        "join",
        (at, *mine, *theirs),
        [SCALARS] + [fixed(a) for a in (*mine, *theirs)],
        [shape((TILES * rows, 2 * cols), F32)],
        [pl.BlockSpec((rows, 2 * cols), lambda i: (i, 0))],
        (TILES,),
    )[0]


def swap(value, axis, offset):
    size = lax.axis_size(axis)
    return lax.ppermute(value, axis, [(i, i ^ offset) for i in range(size)])


def offsets_of(size):
    order = [0]
    step = size // 2
    while step:
        order += [o ^ step for o in order]
        step //= 2
    return order


def tie(values, others):
    return lax.optimization_barrier((values, others))[0]


def swaps(moves, first=(), beside=()):
    sent = tie([m[0] for m in moves], list(first))
    got = [swap(v, *where) for v, (_, *where) in zip(sent, moves)]
    return lax.optimization_barrier((got, list(beside)))[0]


class CtxSums:
    GAP = 2

    def __init__(self, block):
        self.length = lax.axis_size("ctx") // 2
        self.depth = self.length // 2 - 1
        self.place = lax.axis_index("ctx") // 2
        self.number = 0
        self.own, self.other = {}, {}
        self.final = self.own if self.depth != 1 else {}
        self.got, self.arrived = [], []
        ends = (self.place == 0) | (self.place == self.length - 1)
        self.flag = ends.astype(jnp.int32)[None]
        self.sums, self.sends = {}, {}
        self.own[0] = block
        self.moves = self.plan(0)

    def send(self, value, pairs):
        return lax.ppermute(
            value, "ctx", [(2 * i + y, 2 * j + y) for i, j in pairs for y in range(2)]
        )

    def plan(self, now):
        if self.depth == 1:
            return self.short_plan(now)
        last, own = self.length - 1, self.own
        moves = []
        for j in range(self.depth):
            going, coming = now - self.GAP * j, now - self.GAP * (2 * self.depth - j)
            inward = [(j, j + 1), (last - j, last - j - 1)]
            outward = [(b, a) for a, b in inward]
            outer = (self.place == j) | (self.place == last - j)
            if going in own and coming in own:
                value = jnp.where(outer, own[going], own[coming])
                moves.append((value, inward + outward, going, coming, outer))
            elif going in own:
                moves.append((own[going], inward, going, None, outer))
            elif coming in own:
                moves.append((own[coming], outward, None, coming, outer))
        b = now - self.GAP * self.depth
        if b in own:
            across = [(self.depth, self.depth + 1), (self.depth + 1, self.depth)]
            moves.append((own[b], across, b, None, None))
        b = now - self.GAP * (2 * self.depth + 1)
        if b in own:
            moves.append((own[b], None, b, None, None))
        return moves

    def short_plan(self, now):
        own, ends, middle = self.own, [(0, 1), (3, 2)], [(1, 2), (2, 1)]
        entering, leaving = now in own, now - 2 * self.GAP in own
        moves = []
        if entering and not leaving:
            self.sends[now] = own[now]
        if entering or leaving:
            pairs = (ends if entering else []) + ([(b, a) for a, b in ends] if leaving else [])
            moves.append((self.sends[now], pairs, "ends", now, None))
        if now - self.GAP in own:
            moves.append((self.sums[now - self.GAP], middle, "middle", now, None))
        if now - 3 * self.GAP in own:
            b = now - 3 * self.GAP
            moves.append((self.final[b], None, b, None, None))
        return moves

    def short_settle(self):
        now, ends, middle = None, None, None
        for got, (_, pairs, kind, at, _) in self.arrived:
            if pairs is None:
                self.other[kind] = got
                continue
            now = at
            if kind == "ends":
                ends = got
            else:
                middle = got
        self.arrived = []
        if now is None:
            return
        own = self.own
        fresh, went = own.get(now + self.GAP), own.get(now)
        summed, sent = self.sums.get(now - self.GAP), self.sends.get(now)
        if went is not None and middle is None and fresh is not None:
            self.sums[now] = (went.astype(F32) + ends.astype(F32)).astype(BF)
            return
        fill = next(a for a in (ends, middle) if a is not None)
        arrays = [fill if a is None else a for a in (fresh, went, ends, summed, middle, sent)]
        self.sums[now], self.sends[now + self.GAP], self.final[now - 2 * self.GAP] = relay(
            self.flag, arrays
        )

    def settle(self):
        if self.depth == 1:
            return self.short_settle()
        own = self.own
        for got, (_, pairs, going, coming, outer) in self.arrived:
            if pairs is None:
                self.other[going] = got
                continue
            if going is not None:
                own[going] = (own[going].astype(F32) + got.astype(F32)).astype(BF)
            if coming is not None:
                own[coming] = jnp.where(outer, got, own[coming])
        self.arrived = []

    def slot(self, first=(), extra=(), upcoming=None, beside=()):
        now, moves = self.number, self.moves
        self.number += 1
        sent, more = tie(([m[0] for m in moves], [e[0] for e in extra]), (self.got, list(first)))
        got = [
            swap(value, "ctx", 1) if pairs is None else self.send(value, pairs)
            for value, (_, pairs, *_) in zip(sent, moves)
        ]
        got += [swap(value, *where) for value, (_, *where) in zip(more, extra)]
        if upcoming is not None:
            self.own[now + 1] = upcoming()
        self.settle()
        self.moves = self.plan(now + 1)
        got, ready, _ = lax.optimization_barrier((got, [m[0] for m in self.moves], list(beside)))
        self.moves = [(v, *m[1:]) for v, m in zip(ready, self.moves)]
        self.got = got
        self.arrived = list(zip(got, moves))
        return got[len(moves) :]

    def exchanged(self, block):
        if block in self.other:
            return self.other[block]
        for got, (_, pairs, number, *_) in self.arrived:
            if pairs is None and number == block:
                return got
        return None

    def after(self, values):
        return tie(values, self.got)


def shards(
    tokens,
    block_pair,
    gain_attn,
    w_query,
    b_query,
    w_key,
    b_key,
    w_value,
    b_value,
    w_out,
    gain_mlp,
    w_gate,
    w_up,
    w_down,
    cotangent,
):
    n_ctx = lax.axis_size("ctx")
    n_dp = lax.axis_size("dp")
    dp_index = lax.axis_index("dp")
    parity = lax.axis_index("ctx") % 2
    seq_grp, seq_tok, width = tokens.shape
    kv_width = KV_HEADS * HEAD
    rows = seq_grp * seq_tok
    part = w_query.shape[0]
    key_pos = block_positions(block_pair, n_ctx, seq_tok)
    query_pos = lax.dynamic_slice_in_dim(key_pos, lax.axis_index("ctx") * seq_tok, seq_tok)
    table = rope_tables(query_pos)
    qpos = query_pos[:, None]
    kpos = key_pos[None, :]
    at = jnp.stack([parity, dp_index] + [dp_index ^ o for o in offsets_of(n_dp)]).astype(jnp.int32)

    far, close = n_dp // 2, 1
    cuts = [0]
    for item in (gain_attn, gain_mlp, b_query, b_key, b_value):
        cuts.append(cuts[-1] + item.shape[0])
    small = jnp.concatenate([gain_attn, gain_mlp, b_query, b_key, b_value])[None]
    w_kv = jnp.concatenate([w_key, w_value], 1)
    small_x, kv_x, small_c, kv_c = swaps(
        [(small, "dp", far), (w_kv, "dp", far), (small, "dp", close), (w_kv, "dp", close)]
    )
    small_xc, kv_xc = swaps([(small_x, "dp", close), (kv_x, "dp", close)])
    full_kv = [w_kv, kv_x, kv_c, kv_xc]
    gathered = jnp.concatenate([small, small_x, small_c, small_xc], 0).astype(F32)
    picks = at[2:][None, :] == jnp.arange(n_dp, dtype=jnp.int32)[:, None]
    gathered = jnp.sum(jnp.where(picks[:, :, None], gathered[None], 0.0), 1)
    gain_one, gain_two, bias_query, bias_key, bias_value = [
        gathered[:, a:b].reshape(1, -1) for a, b in zip(cuts[:-1], cuts[1:])
    ]
    bias_kv = jnp.concatenate([bias_key, bias_value], 1)

    grad_rows = cotangent.reshape(rows, width)
    inputs = tokens.reshape(rows, width)
    args = (at, inputs, gain_one, bias_kv, table, *full_kv)
    normed_one, kv_own = call(
        functools.partial(norm_kv_kernel, n_dp, seq_grp),
        "norm_kv",
        args,
        [SCALARS] + [whole(a) for a in args[1:]],
        [shape((rows, width), BF), shape((seq_grp, KV_HEADS, seq_tok, 2 * HEAD), BF)],
        flops=4 * rows * width * kv_width,
    )
    kv_all = lax.all_gather(kv_own, "ctx", axis=0, tiled=False)
    query_x, top_y, query_c = swaps(
        [(w_query, "dp", far), (grad_rows, "ctx", 1), (w_query, "dp", close)], [normed_one]
    )
    (query_xc,) = swaps([(query_x, "dp", close)])
    full_query = [w_query, query_x, query_c, query_xc]
    args = (at, normed_one, bias_query, table, *full_query)
    queries = call(
        functools.partial(query_kernel, n_dp),
        "query",
        args,
        [SCALARS] + [whole(a) for a in args[1:]],
        [shape((rows, width), BF)],
        flops=2 * rows * width * width,
    )[0]
    top_x, top_c = swaps(
        [(grad_rows, "dp", far), (grad_rows, "dp", close)], [query_x], [queries]
    )
    attn_vec = attend_forward(queries, kv_all, qpos, kpos)
    top_xc, top_yc = swaps([(top_x, "dp", close), (top_y, "dp", close)], [top_x], [attn_vec])
    tops = [grad_rows, top_x, top_c, top_xc]
    grad_hidden = hidden_back(w_down, tie(tops, attn_vec))
    out_x, out_c, top_xy = swaps(
        [(w_out, "dp", far), (w_out, "dp", close), (top_x, "ctx", 1)], [top_x], [grad_hidden]
    )
    (out_xc,) = swaps([(out_x, "dp", close)])
    full_out = [w_out, out_x, out_c, out_xc]
    args = (at, inputs, attn_vec, gain_two, *full_out)
    middle, normed_two = call(
        functools.partial(out_norm_kernel, n_dp),
        "out_norm",
        args,
        [SCALARS] + [whole(a) for a in args[1:]],
        [shape((rows, width), F32), shape((rows, width), BF)],
        flops=2 * rows * width * width,
    )

    (top_xyc,) = swaps([(top_xy, "dp", close)], [], [normed_two])
    tops += [top_y, top_xy, top_yc, top_xyc]
    grad_hidden_near = hidden_back(w_down, tie(tops[n_dp:], normed_two))
    norm_x, norm_y, norm_c = swaps(
        [(normed_two, "dp", far), (normed_two, "ctx", 1), (normed_two, "dp", close)],
        [],
        [grad_hidden_near],
    )
    (norm_xc,) = swaps([(norm_x, "dp", close)])
    wide_gate, wide_up = w_gate.T, w_up.T
    norm_own = [normed_two, norm_x, norm_c, norm_xc]
    hidden, grad_gate, grad_up = units(grad_hidden, 0, wide_gate, wide_up, norm_own)
    norm_yx, norm_yc = swaps(
        [(norm_y, "dp", far), (norm_y, "dp", close)], [norm_xc], [hidden]
    )
    (norm_yxc,) = swaps([(norm_yx, "dp", close)], [norm_xc], [hidden])
    norms = norm_own + [norm_y, norm_yx, norm_yc, norm_yxc]
    peers = offsets_of(n_dp)[1:]

    def columns(value):
        return [
            (lax.dynamic_slice_in_dim(value, (dp_index ^ o) * part, part, 1), "dp", o) for o in peers
        ]

    def with_own(value, got):
        return jnp.concatenate(
            [lax.dynamic_slice_in_dim(value, dp_index * part, part, 1)] + list(got), 0
        )

    near = units(grad_hidden_near, 0, wide_gate, wide_up, norms[n_dp:])
    down = weight_tiles(at, tops, [hidden, near[0]])
    line = CtxSums(down[0])

    gate_now, up_now = tie((grad_gate, grad_up), down)
    partial, sent = rows_back([gate_now, up_now], [wide_gate, wide_up])
    normed_cols = line.slot(down, columns(normed_one), lambda: down[1], [partial])
    normed_cols = with_own(normed_one, normed_cols)
    gn_got, *attn_cols = line.slot(
        [partial, sent], [(sent, "dp", close)] + columns(attn_vec), lambda: down[2]
    )
    attn_cols = with_own(attn_vec, attn_cols)
    partial = partial + gn_got.astype(F32)
    sent = partial[rows:].astype(BF)
    gate_now, near_now = line.after((grad_gate, near[1]))
    gate = weight_tiles(at, norms, [gate_now, near_now])
    (gn_got,) = line.slot([sent], [(sent, "dp", far)], lambda: down[3])
    grad_norm_two = partial[:rows] + gn_got.astype(F32)

    args = (at, grad_norm_two, middle, grad_rows, gain_two, *full_out)
    grad_middle, grad_branch, grad_attn, grad_gain_m = call(
        functools.partial(middle_back_kernel, n_dp),
        "middle_back",
        args,
        [SCALARS] + [whole(a) for a in args[1:]],
        [
            shape((rows, width), F32),
            shape((rows, width), BF),
            shape((rows, width), BF),
            shape((1, width), F32),
        ],
        flops=2 * rows * width * width,
    )
    grad_query, grad_kv_all = attend_backward(queries, kv_all, grad_attn, qpos, kpos, table)
    recv = lax.psum_scatter(grad_kv_all, "ctx", scatter_dimension=0, tiled=False)
    line.slot(gate, [], lambda: gate[0])
    (branch_x,) = line.slot([grad_query], [(grad_branch, "dp", far)], lambda: gate[1])
    branches = [jnp.concatenate([grad_branch, branch_x], 0)]
    up_now, near_now = line.after((grad_up, near[2]))
    up = weight_tiles(at, norms, [up_now, near_now])
    query_x, got = line.slot(
        branches, [(grad_query, "dp", far), (branches[0], "dp", close)], lambda: gate[2]
    )
    branches.append(got)
    queries_back = [jnp.concatenate([grad_query, query_x], 0)]
    mlp_partial, mlp_sent = rows_back([tie(hidden, (up, line.got))], [w_down])
    (got,) = line.slot(
        [*up, *queries_back], [(queries_back[0], "dp", close)], lambda: gate[3]
    )
    queries_back.append(got)
    grad_kv = call(
        grad_kv_kernel,
        "grad_kv",
        (recv, table),
        [whole(recv), whole(table)],
        [shape((rows, 2 * kv_width), BF)],
    )[0]
    (mlp_got,) = line.slot([mlp_partial, mlp_sent], [(mlp_sent, "dp", close)], lambda: up[0])
    mlp_partial = mlp_partial + mlp_got.astype(F32)
    mlp_sent = mlp_partial[rows:].astype(BF)
    kvs = line.slot([grad_kv], [(grad_kv, "dp", o) for o in peers], lambda: up[1])
    kvs = [grad_kv, *kvs]
    args = (at, grad_query, grad_kv, inputs, gain_one, grad_middle, *full_query, *full_kv)
    grad_input, grad_gain_a, grad_bias = call(
        functools.partial(input_back_kernel, n_dp),
        "input_back",
        args,
        [SCALARS] + [whole(a) for a in args[1:]],
        [shape((rows, width), F32), shape((1, width), F32), shape((1, width + 2 * kv_width), F32)],
        flops=2 * rows * width * (width + 2 * kv_width),
        scratch=[pltpu.VMEM((rows, width), F32)],
    )
    vectors = jnp.concatenate(
        [
            v.reshape(n_dp, -1)
            for v in (
                grad_gain_a,
                grad_gain_m,
                grad_bias[:, :width],
                grad_bias[:, width : width + kv_width],
                grad_bias[:, width + kv_width :],
            )
        ],
        1,
    )
    shares = [lax.dynamic_slice_in_dim(vectors, at[2 + p], 1, 0) for p in range(n_dp)]
    tile_rows = down[0].shape[0]
    out_keep, query_keep, out_send, query_send = attention_weights(
        at, tile_rows, attn_cols, normed_cols, branches, queries_back, kvs
    )
    got = line.slot(
        [grad_input, *shares], [(s, "dp", o) for s, o in zip(shares[1:], peers)], lambda: up[2]
    )
    share = sum(got, shares[0])
    share_half = cuts[-1] // 2

    def with_share(block, which):
        own = lax.dynamic_slice_in_dim(share, which * share_half, share_half, 1).astype(BF)
        below = tile_rows - part
        own = jnp.pad(own, ((0, below - 1), (0, width // 2 - share_half)))
        return jnp.concatenate([block, own], 0)

    query_keep, query_send = with_share(query_keep, parity), with_share(query_send, 1 - parity)
    (got,) = line.slot([out_keep, out_send], [(out_send, "ctx", 1)], lambda: up[3])
    out_block = (out_keep.astype(F32) + got.astype(F32)).astype(BF)

    def sides(first):
        numbers = range(first, first + TILES)
        return [[line.final[i] for i in numbers], [line.exchanged(i) for i in numbers]]

    full = {}

    def join_next():
        first = len(full) * TILES
        if len(full) == 3 or line.exchanged(first + TILES - 1) is None:
            return []
        full[len(full)] = join(at, *line.after(sides(first)))
        return [full[len(full) - 1]]

    joined = join_next()
    (got,) = line.slot([query_keep, query_send], [(query_send, "ctx", 1)], lambda: out_block)
    query_block = (query_keep.astype(F32) + got.astype(F32)).astype(BF)
    (mlp_got,) = line.slot([*joined, mlp_sent], [(mlp_sent, "dp", far)], lambda: query_block)
    layer_out = (line.after(middle) + mlp_partial[:rows] + mlp_got.astype(F32)).astype(BF)
    layer_out = layer_out.reshape(tokens.shape)
    last = 3 * TILES + 1

    def both(block, mine, theirs):
        mine, theirs = mine.astype(F32), theirs.astype(F32)
        return jnp.where(parity == 0, mine, theirs), jnp.where(parity == 0, theirs, mine)

    while last not in line.other:
        beside = [] if line.number != 3 * TILES + 1 else [layer_out]
        beside += join_next()
        if line.moves:
            line.slot(beside=beside)
        else:
            line.settle()
    while len(full) < 3:
        join_next()
    grad_w_down, grad_w_gate, grad_w_up = [full[i] for i in range(3)]
    pairs = [both(b, line.final[b], line.other[b]) for b in (last - 1, last)]
    grad_w_out = jnp.concatenate([p[:part] for p in pairs[0]], 1)
    grad_w_query = jnp.concatenate([p[:part] for p in pairs[1]], 1)
    share = jnp.concatenate([p[part : part + 1, :share_half] for p in pairs[1]], 1)
    pieces = width // 2 // kv_width
    kv_rows = part // pieces
    grad_w_kv = [
        jnp.concatenate(
            [p[part : part + kv_rows, j * kv_width : (j + 1) * kv_width] for j in range(pieces)], 0
        )
        for p in pairs[0]
    ]
    grad_w_kv = jnp.concatenate(grad_w_kv, 1)

    shares = [share[0, a:b] for a, b in zip(cuts[:-1], cuts[1:])]
    return (
        layer_out,
        grad_input.reshape(tokens.shape),
        shares[0],
        grad_w_query,
        shares[2],
        grad_w_kv[:, :kv_width],
        shares[3],
        grad_w_kv[:, kv_width:],
        shares[4],
        grad_w_out,
        shares[1],
        grad_w_gate.T,
        grad_w_up.T,
        grad_w_down,
    )


def solution(mesh):
    placed = (
        P("dp", "ctx", None),
        P(),
        P("dp"),
        P("dp", None),
        P("dp"),
        P("dp", None),
        P("dp"),
        P("dp", None),
        P("dp"),
        P("dp", None),
        P("dp"),
        P(None, "dp"),
        P(None, "dp"),
        P("dp", None),
        P("dp", "ctx", None),
    )
    return jax.shard_map(
        shards,
        mesh=mesh,
        in_specs=placed,
        out_specs=(
            P("dp", "ctx", None),
            P("dp", "ctx", None),
            P("dp"),
            P("dp", None),
            P("dp"),
            P("dp", None),
            P("dp"),
            P("dp", None),
            P("dp"),
            P("dp", None),
            P("dp"),
            P(None, "dp"),
            P(None, "dp"),
            P("dp", None),
        ),
        check_vma=False,
    )
```
